512 devices in a mesh: mem: 16 (over z_hi, y), reg: 32 (over x, z_lo, core).
Axes of the slice: x: 4, y: 4, z: 16 (z_hi: 4, z_lo: 4; z = z_hi * 4 + z_lo), core: 2. Of those that a mesh axis runs over, the one named last changes fastest.
Arguments:
- alpha: float32 [128, 16, 128, 128], P('mem', None, 'reg'), may hold values from -6 to 6
- perturbation: bfloat16 [128, 2, 16, 512, 512], P('mem', None, None, 'reg'), may hold values from -6 to 6
- obs_cell: int32 [32768], P('reg'), may hold values from 0 to 131071
- obs_kind: int32 [32768], P('reg'), may hold values from 0 to 3
- obs_value: float32 [32768], P('reg'), may hold values from -6 to 6
- obs_weight: float32 [32768], P('reg'), may hold values from 1 to 4
Outputs:
- obs_gradient: float32 [128, 16, 128, 128], P('mem', None, 'reg')
The draws below stay inside these ranges and needn't reach their ends.
Inputs may be any that keep to these rules, and one draw needn't show every extreme that they name: `obs_cell`: each entry is level * 16 * 512 + row * 512 + column of a fine cell, the row counted from the first row of the observation's own region. `obs_kind`: 0 zonal wind, 1 meridional wind, 2 relative vorticity, 3 zonal wind advection.
All inputs are finite; a program needn't handle non-finite values.
Results may differ from the reference program's by a relative error of at most 0.0003.
Values sent between devices are 32-bit elements; how exact they have to be, the bound alone decides.
A program may use at most 64 MiB of HBM per device.

```python
import math
import jax
import jax.numpy as jnp
from jax import lax

RX = 16
NY = 512
LEV = 16
OBS_REG = 1024
PASSES = 2
MEMBERS = 128
NX = 512
NXC = 128
NYC = 128
OBS = 32768


def touch_ends(entries, own_key, least, top_value):
    longest = entries.shape.index(max(entries.shape))
    spots = []
    for shift in (0, 1):
        where = [jax.random.randint(jax.random.fold_in(own_key, axis), (), 0, length) for axis, length in enumerate(entries.shape)]
        where[longest] = (where[longest] + shift) % entries.shape[longest]
        spots.append(tuple(where))
    return entries.at[spots[0]].set(least).at[spots[1]].set(top_value)


def spiked(entries, key, source, target, parts, factor):
    owner, partner = [(jnp.arange(entries.shape[position]) // (entries.shape[position] // parts)).reshape([-1 if axis == position else 1 for axis in range(entries.ndim)]) for position in (source, target)]
    chosen = jax.random.permutation(key, parts)[partner]
    strong = (owner == chosen) | (owner == (partner + parts // 2) % parts)
    return jnp.where(strong, factor * entries, entries)


def block_scale(key, extent, cuts, smallest, top_value):
    def one(position, parts):
        steps = jax.random.uniform(jax.random.fold_in(jax.random.fold_in(key, 6), position), (parts,), jnp.float32, smallest / len(cuts), top_value / len(cuts))
        return jnp.repeat(jnp.exp(steps), extent[position] // parts).reshape((-1,) + (1,) * (len(extent) - position - 1))

    level = one(*cuts[0])
    for cut in cuts[1:]:
        level = level * one(*cut)
    return level


def bell_draw(rng, dims, width, most, pieces=(), held_as=jnp.bfloat16):
    array = width * jax.random.normal(rng, dims, jnp.float32)
    if pieces:
        array = array * block_scale(rng, dims, pieces, -0.22, 0.18)
    return jnp.clip(array, -most, most).astype(held_as)


def noise_with(key, extent, width, reach, shards, heavy, held_as=jnp.bfloat16):
    array = width * jax.random.normal(key, extent, jnp.float32)
    if shards:
        array = array * block_scale(key, extent, shards, -0.22, 0.18)
    return jnp.clip(spiked(array, jax.random.fold_in(key, 3), *heavy), -reach, reach).astype(held_as)


def setup_inputs(seed: int = 0) -> dict:
    seeds = jax.random.split(jax.random.key(seed), 7)
    alpha = bell_draw(seeds[0], (MEMBERS, LEV, NXC, NYC), 1.0, 6.0, ((0, 16), (2, 32)), jnp.float32)
    perturbation = noise_with(seeds[1], (MEMBERS, 2, LEV, NX, NY), 1.0, 6.0, ((0, 16), (3, 32)), (0, 2, 16, 2.0))
    obs_cell = touch_ends(jax.random.randint(seeds[2], (OBS,), 0, LEV * RX * NY), jax.random.fold_in(seeds[2], 1), 0, (LEV * RX * NY) - 1).astype(jnp.int32)
    obs_kind = touch_ends(jax.random.randint(seeds[3], (OBS,), 0, 4), jax.random.fold_in(seeds[3], 1), 0, 3).astype(jnp.int32)
    obs_value = bell_draw(seeds[4], (OBS,), 1.0, 6.0, ((0, 32),), jnp.float32)
    obs_weight = jnp.clip(jnp.exp(math.log(4.0) - 1.3862944 * jax.random.uniform(seeds[5], (OBS,), jnp.float32) ** block_scale(seeds[5], (OBS,), ((0, 32),), -0.2, 0.2)), 1.0, 4.0)
    return {"alpha": alpha, "perturbation": perturbation, "obs_cell": obs_cell, "obs_kind": obs_kind, "obs_value": obs_value, "obs_weight": obs_weight}


diffuse = 0.2
highest = lax.Precision.HIGHEST

def weights(fine_rows, fine_start, coarse_count, coarse_start):
    finer = (jnp.arange(fine_rows) + fine_start).astype(jnp.float32)
    coarser = (jnp.arange(coarse_count) + coarse_start).astype(jnp.float32)
    where_at = (finer[:, None] + 0.5) / 4.0 - 0.5
    return jnp.maximum(0.0, 1.0 - jnp.abs(where_at - coarser[None, :]))

def one_pass(block):
    padded = jnp.pad(block, ((0, 0), (0, 0), (1, 1), (1, 1)))
    beside_all = padded[:, :, 2:, 1:-1] + padded[:, :, :-2, 1:-1] + padded[:, :, 1:-1, 2:] + padded[:, :, 1:-1, :-2]
    return block + diffuse * (beside_all - 4.0 * block)

def slopes(padded):
    along_x = (padded[..., 2:, 1:-1] - padded[..., :-2, 1:-1]) * 0.5
    along_y = (padded[..., 1:-1, 2:] - padded[..., 1:-1, :-2]) * 0.5
    return (along_x, along_y)

def reference(alpha, perturbation, obs_cell, obs_kind, obs_value, obs_weight):
    members = alpha.shape[0]
    scale = 1.0 / math.sqrt(members)
    rows_x = weights(NX, 0, NXC, 0)
    rows_y = weights(NY, 0, NYC, 0)
    smooth = alpha
    for step in range(PASSES):
        smooth = one_pass(smooth)

    def accumulate(total, item):
        coarse_one, pert = item
        part = jnp.einsum('ia,lab->lib', rows_x, coarse_one, precision=highest)
        fine = jnp.einsum('lib,jb->lij', part, rows_y, precision=highest)
        return (total + fine[None] * pert.astype(jnp.float32), None)
    total, _ = lax.scan(accumulate, jnp.zeros((2, LEV, NX, NY), jnp.float32), (smooth, perturbation))
    increment = total * scale
    padded = jnp.pad(increment, ((0, 0), (0, 0), (1, 1), (1, 1)))
    zonal_x, zonal_y = slopes(padded[0])
    merid_x, _ = slopes(padded[1])
    zonal = increment[0]
    merid = increment[1]
    fields = jnp.stack([zonal, merid, merid_x - zonal_y, zonal * zonal_x + merid * zonal_y])
    region = (jnp.arange(OBS) // OBS_REG).astype(jnp.int32)
    level = obs_cell // (RX * NY)
    rest = obs_cell % (RX * NY)
    row_in = rest // NY
    column = rest % NY
    flat = obs_kind * (LEV * NX * NY) + level * (NX * NY) + (region * RX + row_in) * NY + column
    seen = fields.reshape(-1)[flat]
    misfit = obs_weight * (seen - obs_value)
    adjoint = jax.ops.segment_sum(misfit, flat, num_segments=4 * LEV * NX * NY).reshape(4, LEV, NX, NY)
    carried = jnp.stack([adjoint[2], adjoint[3] * zonal, adjoint[3] * merid])
    back = jnp.pad(carried, ((0, 0), (0, 0), (1, 1), (1, 1)))
    vort_x, vort_y = slopes(back[0])
    flux_x, _ = slopes(back[1])
    _, flux_y = slopes(back[2])
    grad_u = adjoint[0] + adjoint[3] * zonal_x + vort_y - flux_x - flux_y
    grad_v = adjoint[1] + adjoint[3] * zonal_y - vort_x
    grad_fine = jnp.stack([grad_u, grad_v])

    def project(pert):
        product = lax.optimization_barrier(jnp.sum(pert.astype(jnp.float32) * grad_fine, axis=0))
        part = jnp.einsum('lij,jb->lib', product, rows_y, precision=highest)
        return jnp.einsum('ia,lib->lab', rows_x, part, precision=highest) * scale
    gradient = lax.map(project, perturbation)
    for step in range(PASSES):
        gradient = one_pass(gradient)
    return gradient
```

```python
import functools
import math

import jax
import jax.numpy as jnp
from jax import lax
from jax.experimental import pallas as pl
from jax.experimental.pallas import tpu as pltpu
from jax.sharding import PartitionSpec as P

MESH = pl.DeviceIdType.MESH
F32, BF16, I32 = jnp.float32, jnp.bfloat16, jnp.int32
diffuse = 0.2

YS = 4
ZS = 4
M, L, R, C = 8, 16, 4, 128
RX, NY, OBS = 16, 512, 1024
LINES = L * RX
NT = (((1,), (1,)), ((), ()))


def split(value):
    high = value.astype(BF16)
    return high, (value - high.astype(F32)).astype(BF16)


def dot(a, b):
    return jnp.dot(a, b, preferred_element_type=F32)


def dot_nt(a, b):
    return lax.dot_general(a, b, NT, preferred_element_type=F32)


def sides(value):
    lane = lax.broadcasted_iota(I32, value.shape, 1)
    left = jnp.where(lane == 0, 0.0, pltpu.roll(value, 1, 1))
    right = jnp.where(lane == C - 1, 0.0, pltpu.roll(value, C - 1, 1))
    return left + right


def one_pass(rows, first, last, inside):
    out = {}
    for k in range(first, last + 1):
        here, above, below = rows.get(k), rows.get(k - 1), rows.get(k + 1)
        vertical = [v for v in (above, below) if v is not None]
        beside = vertical[0] if len(vertical) == 1 else vertical[0] + vertical[1] if vertical else None
        if here is not None:
            beside = sides(here) if beside is None else beside + sides(here)
            value = here + diffuse * (beside - 4.0 * here)
        else:
            value = diffuse * beside
        out[k] = inside(k, value)
    return out


def kernel(
    scale,
    regions,
    alpha_hbm,
    pert_hbm,
    cell_ref,
    kind_ref,
    val_ref,
    wt_ref,
    out_ref,
    pert,
    alpha,
    slab,
    part,
    c0t,
    c1t,
    r0f,
    r1f,
    r0b,
    r1b,
    py2,
    pyt,
    thi,
    tlo,
    etop,
    ebot,
    rtop,
    rbot,
    ysend,
    yrecv,
    zsend,
    zrecv,
    zfar,
    lc,
    lh,
    ftop,
    fbot,
    gtop,
    gbot,
    grad,
    own,
    sup,
    sdn,
    qup,
    qdn,
    local_sem,
    send_sem,
    recv_sem,
):
    mem = lax.axis_index("mem")
    reg = lax.axis_index("reg")
    y, zh = lax.rem(mem, YS), mem // YS
    up = lax.rem(reg + 1, regions)
    down = lax.rem(reg + regions - 1, regions)
    has_prev = reg > 0
    has_next = reg < regions - 1
    y_peers = [zh * YS + lax.rem(y + d, YS) for d in range(1, YS)]
    z_up = lax.rem(zh + 1, ZS) * YS + y
    z_down = lax.rem(zh + ZS - 1, ZS) * YS + y

    def send(source, target, index, **where):
        copy = pltpu.make_async_remote_copy(
            src_ref=source,
            dst_ref=target,
            send_sem=send_sem.at[index],
            recv_sem=recv_sem.at[index],
            device_id=where,
            device_id_type=MESH,
        )
        copy.start()
        return copy

    barrier = pltpu.get_barrier_semaphore()
    for who in (up, down):
        pl.semaphore_signal(barrier, inc=1, device_id={"reg": who}, device_id_type=MESH)
    for who in y_peers + [z_up, z_down]:
        pl.semaphore_signal(barrier, inc=1, device_id={"mem": who}, device_id_type=MESH)
    get_alpha = pltpu.make_async_copy(alpha_hbm, alpha, local_sem.at[0])
    get_alpha.start()
    get_pert = pltpu.make_async_copy(pert_hbm, pert, local_sem.at[1])
    get_pert.start()
    get_alpha.wait()
    for r in range(R):
        slab[3 + r] = alpha[pl.ds(r, M * L, stride=R), :]
    pl.semaphore_wait(barrier, 2 + YS - 1 + 2)

    halo_up = send(slab.at[pl.ds(4, 3)], slab.at[pl.ds(0, 3)], 0, reg=up)
    halo_down = send(slab.at[pl.ds(3, 3)], slab.at[pl.ds(7, 3)], 1, reg=down)

    cell = cell_ref[...]
    kind = kind_ref[...]
    column = cell & (NY - 1)
    row_in = (cell >> 9) & (RX - 1)
    level = cell >> 13
    line = cell >> 9
    line_m = jnp.where(row_in > 0, line - 1, LINES + level)
    line_p = jnp.where(row_in < RX - 1, line + 1, LINES + L + level)

    def build_columns(step, _):
        at = pl.multiple_of(step * 32, 32)
        number = lax.broadcasted_iota(I32, (32, OBS), 0) + at
        c0t[pl.ds(at, 32), :] = jnp.where(number == column, 1.0, 0.0).astype(BF16)
        c1t[pl.ds(at, 32), :] = jnp.where(
            number == column + 1, 0.5, jnp.where(number == column - 1, -0.5, 0.0)
        ).astype(BF16)
        return _

    lax.fori_loop(0, NY // 32, build_columns, 0)

    def build_lines(step, _):
        at = pl.multiple_of(step * 32, 32)
        number = lax.broadcasted_iota(I32, (32, OBS), 0) + at
        r0 = jnp.where(number == line, 1.0, 0.0)
        r1 = jnp.where(number == line_p, 0.5, jnp.where(number == line_m, -0.5, 0.0))
        r0f[pl.ds(at, 32), :] = r0
        r1f[pl.ds(at, 32), :] = r1
        r0b[pl.ds(at, 32), :] = r0.astype(BF16)
        r1b[pl.ds(at, 32), :] = r1.astype(BF16)
        return _

    lax.fori_loop(0, (LINES + 2 * L) // 32, build_lines, 0)

    def table(shape, fine_dim):
        fine = lax.broadcasted_iota(I32, shape, fine_dim).astype(F32)
        coarse = lax.broadcasted_iota(I32, shape, 1 - fine_dim).astype(F32)
        return jnp.maximum(0.0, 1.0 - jnp.abs((fine + 0.5) / 4.0 - 0.5 - coarse)).astype(BF16)

    weights = table((C, NY), 1)
    py2[0:C, :] = weights
    py2[C : 2 * C, :] = weights
    pyt[...] = table((NY, C), 0)

    def inside(k, value):
        if k < 0:
            return jnp.where(has_prev, value, 0.0)
        if k >= R:
            return jnp.where(has_next, value, 0.0)
        return value

    halo_up.wait()
    halo_down.wait()

    def smooth_member(m, _):
        at = pl.multiple_of(m * L, L)
        rows = {k - 3: inside(k - 3, slab[k, pl.ds(at, L), :]) for k in range(R + 6)}
        rows = one_pass(rows, -2, R + 1, inside)
        rows = one_pass(rows, -1, R, inside)
        for i in range(RX):
            q, s = divmod(i, 4)
            mine, other = ((0.625, 0.375), (0.875, 0.125), (0.875, 0.125), (0.625, 0.375))[s]
            near = q - 1 if s < 2 else q + 1
            value = mine * rows[q] + other * rows[near]
            part[pl.ds(m * (L * RX) + i, L, stride=RX), :] = value
        return _

    lax.fori_loop(0, M, smooth_member, 0)
    get_pert.wait()

    LB = 2

    def increments(step, _):
        pieces = []
        for k in range(LB):
            for m in range(M):
                at = pl.multiple_of(m * (L * RX) + (step * LB + k) * RX, RX)
                pieces.append(part[pl.ds(at, RX), :])
        high, low = split(jnp.concatenate(pieces, axis=0))
        fine = dot(jnp.concatenate([high, low], axis=1), py2[...])
        for k in range(LB):
            lev = step * LB + k
            for w in range(2):
                total = None
                for m in range(M):
                    at = (k * M + m) * RX
                    term = fine[at : at + RX] * pert[m, w, lev].astype(F32)
                    total = term if total is None else total + term
                at = pl.multiple_of(w * LINES + lev * RX, RX)
                thi[pl.ds(at, RX), :], tlo[pl.ds(at, RX), :] = split(total)
                etop[w, pl.ds(lev, 1), :] = total[0:1]
                ebot[w, pl.ds(lev, 1), :] = total[RX - 1 : RX]
        return _

    lax.fori_loop(0, L // LB, increments, 0)

    edge_down = send(etop, rbot, 2, reg=down)
    edge_up = send(ebot, rtop, 3, reg=up)

    NB = 256

    def pick(step, _):
        at = pl.multiple_of(step * NB, NB)
        near, slope = c0t[:, pl.ds(at, NB)], c1t[:, pl.ds(at, NB)]
        second = kind_ref[:, pl.ds(at, NB)] == 2

        def picked(first, rhs):
            return dot(thi[first : first + LINES, :], rhs) + dot(tlo[first : first + LINES, :], rhs)

        on = r0f[0:LINES, pl.ds(at, NB)]
        at_u = picked(0, near)
        at_v = picked(LINES, near)
        ysend[0:1, pl.ds(at, NB)] = jnp.sum(on * at_u, axis=0, keepdims=True)
        ysend[1:2, pl.ds(at, NB)] = jnp.sum(on * at_v, axis=0, keepdims=True)
        ysend[2:3, pl.ds(at, NB)] = jnp.sum(
            r1f[0:LINES, pl.ds(at, NB)] * jnp.where(second, at_v, at_u), axis=0, keepdims=True
        )
        at_y = picked(0, slope)
        ysend[3:4, pl.ds(at, NB)] = jnp.sum(on * at_y, axis=0, keepdims=True)
        return _

    lax.fori_loop(0, OBS // NB, pick, 0)
    edge_down.wait()
    edge_up.wait()
    rims = []
    for w in range(2):
        rims.append(jnp.where(has_prev, rtop[w], 0.0))
        rims.append(jnp.where(has_next, rbot[w], 0.0))
    high, low = split(jnp.concatenate(rims, axis=0))
    rim = dot(high, c0t[...]) + dot(low, c0t[...])
    rim = jnp.where(kind == 2, rim[2 * L :], rim[: 2 * L])
    ysend[2:3, :] = ysend[2:3, :] + jnp.sum(r1f[LINES:, :] * rim, axis=0, keepdims=True)

    copies = [send(ysend, yrecv.at[d], 4 + d, mem=who) for d, who in enumerate(y_peers)]
    total = ysend[...]
    for d, copy in enumerate(copies):
        copy.wait()
        total = total + yrecv[d]
    zsend[...] = total
    near_up = send(zsend, zrecv.at[0], 8, mem=z_up)
    near_down = send(zsend, zrecv.at[1], 9, mem=z_down)
    near_up.wait()
    far_up = send(zrecv.at[0, pl.ds(0, 2)], zfar.at[pl.ds(0, 2)], 10, mem=z_up)
    near_down.wait()
    far_down = send(zrecv.at[1, pl.ds(2, 2)], zfar.at[pl.ds(2, 2)], 11, mem=z_down)
    total = total + zrecv[0] + zrecv[1]
    far_up.wait()
    far_down.wait()
    total = (total + zfar[...]) * scale

    u, v, slope_x, slope_y = total[0:1], total[1:2], total[2:3], total[3:4]
    is_u, is_v, is_vort, is_adv = kind == 0, kind == 1, kind == 2, kind == 3
    seen = jnp.where(
        is_u,
        u,
        jnp.where(is_v, v, jnp.where(is_vort, slope_x - slope_y, u * slope_x + v * slope_y)),
    )
    misfit = wt_ref[...] * (seen - val_ref[...]) * scale
    zero = jnp.zeros_like(misfit)
    to_u = split(jnp.where(is_u, misfit, jnp.where(is_adv, misfit * slope_x, zero)))
    to_v = split(jnp.where(is_v, misfit, jnp.where(is_adv, misfit * slope_y, zero)))
    along_u = split(jnp.where(is_adv, misfit * u, zero))
    along_v = split(jnp.where(is_vort, misfit, zero))
    across = split(jnp.where(is_vort, -misfit, jnp.where(is_adv, misfit * v, zero)))

    outer = r1b[LINES:, :]
    high = jnp.concatenate([outer * along_u[0], outer * along_v[0]], axis=0)
    low = jnp.concatenate([outer * along_u[1], outer * along_v[1]], axis=0)
    rim = dot_nt(high, c0t[...]) + dot_nt(low, c0t[...])
    for w in range(2):
        ftop[w] = rim[2 * w * L : (2 * w + 1) * L]
        fbot[w] = rim[(2 * w + 1) * L : (2 * w + 2) * L]
    back_down = send(ftop, gbot, 12, reg=down)
    back_up = send(fbot, gtop, 13, reg=up)

    for half in range(2):
        lc[half * LINES : (half + 1) * LINES, :] = (
            r0b[0:LINES, :] * to_u[half] + r1b[0:LINES, :] * along_u[half]
        )
        lc[(2 + half) * LINES : (3 + half) * LINES, :] = (
            r0b[0:LINES, :] * to_v[half] + r1b[0:LINES, :] * along_v[half]
        )
        lh[half * LINES : (half + 1) * LINES, :] = r0b[0:LINES, :] * across[half]

    def scatter(step, _):
        at = pl.multiple_of(step * NB, NB)
        near, slope = c0t[pl.ds(at, NB), :], c1t[pl.ds(at, NB), :]
        grad[0, :, pl.ds(at, NB)] = (
            dot_nt(lc[0:LINES, :], near)
            + dot_nt(lc[LINES : 2 * LINES, :], near)
            + dot_nt(lh[0:LINES, :], slope)
            + dot_nt(lh[LINES : 2 * LINES, :], slope)
        )
        grad[1, :, pl.ds(at, NB)] = dot_nt(lc[2 * LINES : 3 * LINES, :], near) + dot_nt(
            lc[3 * LINES : 4 * LINES, :], near
        )
        return _

    lax.fori_loop(0, NY // NB, scatter, 0)
    back_down.wait()
    back_up.wait()

    def project(step, _):
        pieces = []
        for k in range(LB):
            lev = step * LB + k
            at = pl.multiple_of(lev * RX, RX)
            row = lax.broadcasted_iota(I32, (RX, NY), 0)
            gradients = []
            for w in range(2):
                first = jnp.where(has_prev, gtop[w, pl.ds(lev, 1), :], 0.0)
                last = jnp.where(has_next, gbot[w, pl.ds(lev, 1), :], 0.0)
                gradients.append(
                    grad[w, pl.ds(at, RX), :]
                    + jnp.where(row == 0, first, jnp.where(row == RX - 1, last, 0.0))
                )
            for m in range(M):
                pieces.append(
                    gradients[0] * pert[m, 0, lev].astype(F32)
                    + gradients[1] * pert[m, 1, lev].astype(F32)
                )
        high, low = split(jnp.concatenate(pieces, axis=0))
        out = dot(high, pyt[...]) + dot(low, pyt[...])
        for k in range(LB):
            for m in range(M):
                at = pl.multiple_of(m * (L * RX) + (step * LB + k) * RX, RX)
                first = (k * M + m) * RX
                part[pl.ds(at, RX), :] = out[first : first + RX]
        return _

    lax.fori_loop(0, L // LB, project, 0)

    def spread_member(m, _):
        at = pl.multiple_of(m * L, L)
        f = [part[pl.ds(m * (L * RX) + i, L, stride=RX), :] for i in range(RX)]
        taps = (0.125, 0.375, 0.625, 0.875, 0.875, 0.625, 0.375, 0.125)
        rows = {}
        for q in range(-1, R + 1):
            value = None
            for t, tap in enumerate(taps):
                i = 4 * q - 2 + t
                if 0 <= i < RX:
                    term = tap * f[i]
                    value = term if value is None else value + term
            rows[q] = inside(q, value)
        rows = one_pass(rows, -2, R + 1, inside)
        rows = one_pass(rows, -3, R + 2, inside)
        for k in range(3):
            sdn[k, pl.ds(at, L), :] = rows[k - 3]
            sup[k, pl.ds(at, L), :] = rows[R + k]
        for k in range(R):
            own[k, pl.ds(at, L), :] = rows[k]
        return _

    lax.fori_loop(0, M, spread_member, 0)
    last_down = send(sdn, qdn, 14, reg=down)
    last_up = send(sup, qup, 15, reg=up)
    last_down.wait()
    last_up.wait()
    for r in range(R):
        value = own[r]
        if r < 3:
            value = value + jnp.where(has_prev, qup[r], 0.0)
        if r >= R - 3:
            value = value + jnp.where(has_next, qdn[r - (R - 3)], 0.0)
        out_ref[pl.ds(r, M * L, stride=R), :] = value


def local(regions, members, alpha, perturbation, obs_cell, obs_kind, obs_value, obs_weight):
    any_space = pl.BlockSpec(memory_space=pl.ANY)
    in_vmem = pl.BlockSpec(memory_space=pltpu.VMEM)
    row = (1, OBS)
    edge = pltpu.VMEM((2, L, NY), F32)
    rows3 = pltpu.VMEM((3, M * L, C), F32)
    out = pl.pallas_call(
        functools.partial(kernel, 1.0 / math.sqrt(members), regions),
        out_shape=jax.ShapeDtypeStruct((M * L * R, C), F32),
        in_specs=[any_space, any_space] + [in_vmem] * 4,
        out_specs=in_vmem,
        scratch_shapes=[
            pltpu.VMEM((M, 2, L, RX, NY), BF16),
            pltpu.VMEM((M * L * R, C), F32),
            pltpu.VMEM((R + 6, M * L, C), F32),
            pltpu.VMEM((M * L * RX, C), F32),
            pltpu.VMEM((NY, OBS), BF16),
            pltpu.VMEM((NY, OBS), BF16),
            pltpu.VMEM((LINES + 2 * L, OBS), F32),
            pltpu.VMEM((LINES + 2 * L, OBS), F32),
            pltpu.VMEM((LINES + 2 * L, OBS), BF16),
            pltpu.VMEM((LINES + 2 * L, OBS), BF16),
            pltpu.VMEM((2 * C, NY), BF16),
            pltpu.VMEM((NY, C), BF16),
            pltpu.VMEM((2 * LINES, NY), BF16),
            pltpu.VMEM((2 * LINES, NY), BF16),
            edge,
            edge,
            edge,
            edge,
            pltpu.VMEM((4, OBS), F32),
            pltpu.VMEM((YS - 1, 4, OBS), F32),
            pltpu.VMEM((4, OBS), F32),
            pltpu.VMEM((2, 4, OBS), F32),
            pltpu.VMEM((4, OBS), F32),
            pltpu.VMEM((4 * LINES, OBS), BF16),
            pltpu.VMEM((2 * LINES, OBS), BF16),
            edge,
            edge,
            edge,
            edge,
            pltpu.VMEM((2, LINES, NY), F32),
            pltpu.VMEM((R, M * L, C), F32),
            rows3,
            rows3,
            rows3,
            rows3,
            pltpu.SemaphoreType.DMA((2,)),
            pltpu.SemaphoreType.DMA((16,)),
            pltpu.SemaphoreType.DMA((16,)),
        ],
        compiler_params=pltpu.CompilerParams(
            collective_id=0, has_side_effects=True, vmem_limit_bytes=56 * 1024 * 1024
        ),
    )(
        alpha.reshape(M * L * R, C),
        perturbation,
        obs_cell.reshape(row),
        obs_kind.reshape(row),
        obs_value.reshape(row),
        obs_weight.reshape(row),
    )
    return out.reshape(M, L, R, C)


def solution(mesh):
    regions, groups = mesh.shape["reg"], mesh.shape["mem"]
    return jax.shard_map(
        functools.partial(local, regions, M * groups),
        mesh=mesh,
        in_specs=(
            P("mem", None, "reg", None),
            P("mem", None, None, "reg", None),
            P("reg"),
            P("reg"),
            P("reg"),
            P("reg"),
        ),
        out_specs=P("mem", None, "reg", None),
        check_vma=False,
    )
```

```python
import functools
import math

import jax
import jax.numpy as jnp
from jax import lax
from jax.experimental import pallas as pl
from jax.experimental.pallas import tpu as pltpu
from jax.sharding import PartitionSpec as P

MESH = pl.DeviceIdType.MESH
F32, BF16, I32 = jnp.float32, jnp.bfloat16, jnp.int32
diffuse = 0.2

YS = 4
ZS = 4
M, L, R, C = 8, 16, 4, 128
RX, NY, OBS = 16, 512, 1024
LINES = L * RX
LB = 2
CHUNKS = L // LB
ROWS = LB * M
GROUPS = 4
PER = CHUNKS // GROUPS
EDGE = 2 * (L // GROUPS)
NT = (((1,), (1,)), ((), ()))


def split(value):
    high = value.astype(BF16)
    return high, (value - high.astype(F32)).astype(BF16)


def dot(a, b):
    return jnp.dot(a, b, preferred_element_type=F32)


def dot_nt(a, b):
    return lax.dot_general(a, b, NT, preferred_element_type=F32)


def sides(value):
    lane = lax.broadcasted_iota(I32, value.shape, 1)
    left = jnp.where(lane == 0, 0.0, pltpu.roll(value, 1, 1))
    right = jnp.where(lane == C - 1, 0.0, pltpu.roll(value, C - 1, 1))
    return left + right


def one_pass(rows, first, last, inside):
    out = {}
    for k in range(first, last + 1):
        here, above, below = rows.get(k), rows.get(k - 1), rows.get(k + 1)
        vertical = [v for v in (above, below) if v is not None]
        beside = vertical[0] if len(vertical) == 1 else vertical[0] + vertical[1] if vertical else None
        if here is not None:
            beside = sides(here) if beside is None else beside + sides(here)
            value = here + diffuse * (beside - 4.0 * here)
        else:
            value = diffuse * beside
        out[k] = inside(k, value)
    return out


def kernel(
    scale,
    regions,
    alpha_hbm,
    pert_hbm,
    cell_ref,
    kind_ref,
    val_ref,
    wt_ref,
    out_ref,
    rest_ref,
    pert,
    alpha,
    slab,
    part,
    c0t,
    c1t,
    r0f,
    r1f,
    r0b,
    r1b,
    rimf,
    rimb,
    py2,
    pyt,
    thi,
    tlo,
    etop,
    ebot,
    rtop,
    rbot,
    ysend,
    yrecv,
    zsend,
    zrecv,
    zfar,
    lc,
    lh,
    ftop,
    fbot,
    gtop,
    gbot,
    grad,
    sup,
    sdn,
    qup,
    qdn,
    local_sem,
    send_sem,
    recv_sem,
):
    mem = lax.axis_index("mem")
    reg = lax.axis_index("reg")
    y, zh = lax.rem(mem, YS), mem // YS
    up = lax.rem(reg + 1, regions)
    down = lax.rem(reg + regions - 1, regions)
    has_prev = reg > 0
    has_next = reg < regions - 1
    y_peers = [zh * YS + lax.rem(y + d, YS) for d in range(1, YS)]
    z_up = lax.rem(zh + 1, ZS) * YS + y
    z_down = lax.rem(zh + ZS - 1, ZS) * YS + y

    def remote(source, target, index, **where):
        return pltpu.make_async_remote_copy(
            src_ref=source,
            dst_ref=target,
            send_sem=send_sem.at[index],
            recv_sem=recv_sem.at[index],
            device_id=where,
            device_id_type=MESH,
        )

    def send(*args, **where):
        copy = remote(*args, **where)
        copy.start()
        return copy

    def rims_in(c):
        at = pl.ds(pl.multiple_of(c * ROWS, ROWS), ROWS)
        return (
            remote(slab.at[pl.ds(4, 3), at], slab.at[pl.ds(0, 3), at], c, reg=up),
            remote(slab.at[pl.ds(3, 3), at], slab.at[pl.ds(7, 3), at], CHUNKS + c, reg=down),
        )

    def rims_out(c):
        at = pl.ds(pl.multiple_of(c * ROWS, ROWS), ROWS)
        first = 2 * CHUNKS
        return (
            remote(sdn.at[:, at], qdn.at[:, at], first + c, reg=down),
            remote(sup.at[:, at], qup.at[:, at], first + CHUNKS + c, reg=up),
        )

    def edges(g):
        first = 4 * CHUNKS
        return (
            remote(etop.at[g], rbot.at[g], first + g, reg=down),
            remote(ebot.at[g], rtop.at[g], first + GROUPS + g, reg=up),
        )

    def edges_back(g):
        first = 4 * CHUNKS + 2 * GROUPS
        return (
            remote(ftop.at[g], gbot.at[g], first + g, reg=down),
            remote(fbot.at[g], gtop.at[g], first + GROUPS + g, reg=up),
        )

    sums = 4 * CHUNKS + 4 * GROUPS

    def begin(copies):
        for copy in copies:
            copy.start()

    def finish(copies):
        for copy in copies:
            copy.wait()

    def each(count, body):
        def step(i, _):
            body(i)
            return _

        lax.fori_loop(0, count, step, 0)

    barrier = pltpu.get_barrier_semaphore()
    for who in (up, down):
        pl.semaphore_signal(barrier, inc=1, device_id={"reg": who}, device_id_type=MESH)
    for who in y_peers + [z_up, z_down]:
        pl.semaphore_signal(barrier, inc=1, device_id={"mem": who}, device_id_type=MESH)
    get_alpha = pltpu.make_async_copy(alpha_hbm, alpha, local_sem.at[0])
    get_alpha.start()
    get_pert = pltpu.make_async_copy(pert_hbm, pert, local_sem.at[1])
    get_pert.start()
    get_alpha.wait()

    def arrange(lev):
        at = pl.multiple_of(lev * M, M)
        for r in range(R):
            slab[3 + r, pl.ds(at, M), :] = alpha[pl.ds(lev * R + r, M, stride=L * R), :]

    each(L, arrange)
    pl.semaphore_wait(barrier, 2 + YS - 1 + 2)

    each(CHUNKS, lambda c: begin(rims_in(c)))

    cell = cell_ref[...]
    kind = kind_ref[...]
    column = cell & (NY - 1)
    row_in = (cell >> 9) & (RX - 1)
    level = cell >> 13
    line = cell >> 9
    line_m = jnp.where(row_in > 0, line - 1, -1)
    line_p = jnp.where(row_in < RX - 1, line + 1, -1)
    per = L // GROUPS
    place = (level // per) * EDGE + level % per + jnp.where(kind == 2, per, 0)
    place = jnp.where(row_in == 0, place, GROUPS * EDGE + place)
    place = jnp.where((kind >= 2) & ((row_in == 0) | (row_in == RX - 1)), place, -1)
    number = lax.broadcasted_iota(I32, (2 * GROUPS * EDGE, OBS), 0)
    outer = jnp.where(number == place, jnp.where(row_in == 0, -0.5, 0.5), 0.0)
    rimf[...] = outer
    rimb[...] = outer.astype(BF16)

    def build_columns(step, _):
        at = pl.multiple_of(step * 32, 32)
        number = lax.broadcasted_iota(I32, (32, OBS), 0) + at
        c0t[pl.ds(at, 32), :] = jnp.where(number == column, 1.0, 0.0).astype(BF16)
        c1t[pl.ds(at, 32), :] = jnp.where(
            number == column + 1, 0.5, jnp.where(number == column - 1, -0.5, 0.0)
        ).astype(BF16)
        return _

    lax.fori_loop(0, NY // 32, build_columns, 0)

    def build_lines(step, _):
        at = pl.multiple_of(step * 32, 32)
        number = lax.broadcasted_iota(I32, (32, OBS), 0) + at
        r0 = jnp.where(number == line, 1.0, 0.0)
        r1 = jnp.where(number == line_p, 0.5, jnp.where(number == line_m, -0.5, 0.0))
        r0f[pl.ds(at, 32), :] = r0
        r1f[pl.ds(at, 32), :] = r1
        r0b[pl.ds(at, 32), :] = r0.astype(BF16)
        r1b[pl.ds(at, 32), :] = r1.astype(BF16)
        return _

    lax.fori_loop(0, LINES // 32, build_lines, 0)

    def table(shape, fine_dim):
        fine = lax.broadcasted_iota(I32, shape, fine_dim).astype(F32)
        coarse = lax.broadcasted_iota(I32, shape, 1 - fine_dim).astype(F32)
        return jnp.maximum(0.0, 1.0 - jnp.abs((fine + 0.5) / 4.0 - 0.5 - coarse)).astype(BF16)

    weights = table((C, NY), 1)
    py2[0:C, :] = weights
    py2[C : 2 * C, :] = weights
    pyt[...] = table((NY, C), 0)

    def inside(k, value):
        if k < 0:
            return jnp.where(has_prev, value, 0.0)
        if k >= R:
            return jnp.where(has_next, value, 0.0)
        return value

    get_pert.wait()

    def increments(group):
        for h in range(PER):
            c = group * PER + h
            finish(rims_in(c))
            at = pl.multiple_of(c * ROWS, ROWS)
            rows = {k - 3: inside(k - 3, slab[k, pl.ds(at, ROWS), :]) for k in range(R + 6)}
            rows = one_pass(rows, -2, R + 1, inside)
            rows = one_pass(rows, -1, R, inside)
            at = pl.multiple_of(c * (ROWS * RX), ROWS * RX)
            for i in range(RX):
                q, s = divmod(i, 4)
                mine, other = ((0.625, 0.375), (0.875, 0.125), (0.875, 0.125), (0.625, 0.375))[s]
                near = q - 1 if s < 2 else q + 1
                part[pl.ds(at + i, ROWS, stride=RX), :] = mine * rows[q] + other * rows[near]
            high, low = split(part[pl.ds(at, ROWS * RX), :])
            fine = dot(jnp.concatenate([high, low], axis=1), py2[...])
            for k in range(LB):
                lev = c * LB + k
                for w in range(2):
                    total = None
                    for m in range(M):
                        at = (k * M + m) * RX
                        term = fine[at : at + RX] * pert[m, w, lev].astype(F32)
                        total = term if total is None else total + term
                    at = pl.multiple_of(w * LINES + lev * RX, RX)
                    thi[pl.ds(at, RX), :], tlo[pl.ds(at, RX), :] = split(total)
                    row = w * (EDGE // 2) + h * LB + k
                    etop[group, row : row + 1, :] = total[0:1]
                    ebot[group, row : row + 1, :] = total[RX - 1 : RX]
        begin(edges(group))

    each(GROUPS, increments)

    NB = 256

    def pick(step, _):
        at = pl.multiple_of(step * NB, NB)
        near, slope = c0t[:, pl.ds(at, NB)], c1t[:, pl.ds(at, NB)]
        second = kind_ref[:, pl.ds(at, NB)] == 2

        def picked(first, rhs):
            return dot(thi[first : first + LINES, :], rhs) + dot(tlo[first : first + LINES, :], rhs)

        on = r0f[0:LINES, pl.ds(at, NB)]
        at_u = picked(0, near)
        at_v = picked(LINES, near)
        ysend[0:1, pl.ds(at, NB)] = jnp.sum(on * at_u, axis=0, keepdims=True)
        ysend[1:2, pl.ds(at, NB)] = jnp.sum(on * at_v, axis=0, keepdims=True)
        ysend[2:3, pl.ds(at, NB)] = jnp.sum(
            r1f[0:LINES, pl.ds(at, NB)] * jnp.where(second, at_v, at_u), axis=0, keepdims=True
        )
        at_y = picked(0, slope)
        ysend[3:4, pl.ds(at, NB)] = jnp.sum(on * at_y, axis=0, keepdims=True)
        return _

    lax.fori_loop(0, OBS // NB, pick, 0)
    each(GROUPS, lambda g: finish(edges(g)))
    sides_in = [
        jnp.where(has_prev, rtop[...].reshape(GROUPS * EDGE, NY), 0.0),
        jnp.where(has_next, rbot[...].reshape(GROUPS * EDGE, NY), 0.0),
    ]
    high, low = split(jnp.concatenate(sides_in, axis=0))
    rim = dot(high, c0t[...]) + dot(low, c0t[...])
    ysend[2:3, :] = ysend[2:3, :] + jnp.sum(rimf[...] * rim, axis=0, keepdims=True)

    copies = [send(ysend, yrecv.at[d], sums + d, mem=who) for d, who in enumerate(y_peers)]
    total = ysend[...]
    for d, copy in enumerate(copies):
        copy.wait()
        total = total + yrecv[d]
    zsend[...] = total
    near_up = send(zsend, zrecv.at[0], sums + 3, mem=z_up)
    near_down = send(zsend, zrecv.at[1], sums + 4, mem=z_down)
    near_up.wait()
    far_up = send(zrecv.at[0, pl.ds(0, 2)], zfar.at[pl.ds(0, 2)], sums + 5, mem=z_up)
    near_down.wait()
    far_down = send(zrecv.at[1, pl.ds(2, 2)], zfar.at[pl.ds(2, 2)], sums + 6, mem=z_down)
    total = total + zrecv[0] + zrecv[1]
    far_up.wait()
    far_down.wait()
    total = (total + zfar[...]) * scale

    u, v, slope_x, slope_y = total[0:1], total[1:2], total[2:3], total[3:4]
    is_u, is_v, is_vort, is_adv = kind == 0, kind == 1, kind == 2, kind == 3
    seen = jnp.where(
        is_u,
        u,
        jnp.where(is_v, v, jnp.where(is_vort, slope_x - slope_y, u * slope_x + v * slope_y)),
    )
    misfit = wt_ref[...] * (seen - val_ref[...]) * scale
    zero = jnp.zeros_like(misfit)
    to_u = split(jnp.where(is_u, misfit, jnp.where(is_adv, misfit * slope_x, zero)))
    to_v = split(jnp.where(is_v, misfit, jnp.where(is_adv, misfit * slope_y, zero)))
    along_u = split(jnp.where(is_adv, misfit * u, zero))
    along_v = split(jnp.where(is_vort, misfit, zero))
    across = split(jnp.where(is_vort, -misfit, jnp.where(is_adv, misfit * v, zero)))

    high = rimb[...] * (along_u[0] + along_v[0])
    low = rimb[...] * (along_u[1] + along_v[1])
    rim = dot_nt(high, c0t[...]) + dot_nt(low, c0t[...])
    ftop[...] = rim[: GROUPS * EDGE].reshape(GROUPS, EDGE, NY)
    fbot[...] = rim[GROUPS * EDGE :].reshape(GROUPS, EDGE, NY)
    each(GROUPS, lambda g: begin(edges_back(g)))

    for half in range(2):
        lc[half * LINES : (half + 1) * LINES, :] = (
            r0b[0:LINES, :] * to_u[half] + r1b[0:LINES, :] * along_u[half]
        )
        lc[(2 + half) * LINES : (3 + half) * LINES, :] = (
            r0b[0:LINES, :] * to_v[half] + r1b[0:LINES, :] * along_v[half]
        )
        lh[half * LINES : (half + 1) * LINES, :] = r0b[0:LINES, :] * across[half]

    def scatter(step, _):
        at = pl.multiple_of(step * NB, NB)
        near, slope = c0t[pl.ds(at, NB), :], c1t[pl.ds(at, NB), :]
        grad[0, :, pl.ds(at, NB)] = (
            dot_nt(lc[0:LINES, :], near)
            + dot_nt(lc[LINES : 2 * LINES, :], near)
            + dot_nt(lh[0:LINES, :], slope)
            + dot_nt(lh[LINES : 2 * LINES, :], slope)
        )
        grad[1, :, pl.ds(at, NB)] = dot_nt(lc[2 * LINES : 3 * LINES, :], near) + dot_nt(
            lc[3 * LINES : 4 * LINES, :], near
        )
        return _

    lax.fori_loop(0, NY // NB, scatter, 0)

    def project(group):
        finish(edges_back(group))
        for h in range(PER):
            c = group * PER + h
            pieces = []
            row = lax.broadcasted_iota(I32, (RX, NY), 0)
            for k in range(LB):
                lev = c * LB + k
                at = pl.multiple_of(lev * RX, RX)
                gradients = []
                for w in range(2):
                    edge = w * (EDGE // 2) + h * LB + k
                    first = jnp.where(has_prev, gtop[group, edge : edge + 1, :], 0.0)
                    last = jnp.where(has_next, gbot[group, edge : edge + 1, :], 0.0)
                    gradients.append(
                        grad[w, pl.ds(at, RX), :]
                        + jnp.where(row == 0, first, jnp.where(row == RX - 1, last, 0.0))
                    )
                for m in range(M):
                    pieces.append(
                        gradients[0] * pert[m, 0, lev].astype(F32)
                        + gradients[1] * pert[m, 1, lev].astype(F32)
                    )
            high, low = split(jnp.concatenate(pieces, axis=0))
            at = pl.multiple_of(c * (ROWS * RX), ROWS * RX)
            part[pl.ds(at, ROWS * RX), :] = dot(high, pyt[...]) + dot(low, pyt[...])
            f = [part[pl.ds(at + i, ROWS, stride=RX), :] for i in range(RX)]
            taps = (0.125, 0.375, 0.625, 0.875, 0.875, 0.625, 0.375, 0.125)
            rows = {}
            for q in range(-1, R + 1):
                value = None
                for t, tap in enumerate(taps):
                    i = 4 * q - 2 + t
                    if 0 <= i < RX:
                        term = tap * f[i]
                        value = term if value is None else value + term
                rows[q] = inside(q, value)
            rows = one_pass(rows, -2, R + 1, inside)
            rows = one_pass(rows, -3, R + 2, inside)
            at = pl.multiple_of(c * ROWS, ROWS)
            for k in range(3):
                sdn[k, pl.ds(at, ROWS), :] = rows[k - 3]
                sup[k, pl.ds(at, ROWS), :] = rows[R + k]
            for k in range(LB):
                for r in range(R):
                    out_ref[pl.ds((c * LB + k) * R + r, M, stride=L * R), :] = rows[r][
                        k * M : (k + 1) * M
                    ]
            begin(rims_out(c))

    each(GROUPS, project)

    def collect(c):
        finish(rims_out(c))
        for k in range(LB):
            at = pl.multiple_of(c * ROWS + k * M, M)
            for r in range(R):
                value = 0.0
                if r < 3:
                    value = value + jnp.where(has_prev, qup[r, pl.ds(at, M), :], 0.0)
                if r >= R - 3:
                    value = value + jnp.where(has_next, qdn[r - (R - 3), pl.ds(at, M), :], 0.0)
                rest_ref[pl.ds((c * LB + k) * R + r, M, stride=L * R), :] = value

    each(CHUNKS, collect)


def local(regions, members, alpha, perturbation, obs_cell, obs_kind, obs_value, obs_weight):
    any_space = pl.BlockSpec(memory_space=pl.ANY)
    in_vmem = pl.BlockSpec(memory_space=pltpu.VMEM)
    row = (1, OBS)
    edge = pltpu.VMEM((GROUPS, EDGE, NY), F32)
    rows3 = pltpu.VMEM((3, M * L, C), F32)
    out, rest = pl.pallas_call(
        functools.partial(kernel, 1.0 / math.sqrt(members), regions),
        out_shape=[jax.ShapeDtypeStruct((M * L * R, C), F32)] * 2,
        in_specs=[any_space, any_space] + [in_vmem] * 4,
        out_specs=[in_vmem] * 2,
        scratch_shapes=[
            pltpu.VMEM((M, 2, L, RX, NY), BF16),
            pltpu.VMEM((M * L * R, C), F32),
            pltpu.VMEM((R + 6, M * L, C), F32),
            pltpu.VMEM((M * L * RX, C), F32),
            pltpu.VMEM((NY, OBS), BF16),
            pltpu.VMEM((NY, OBS), BF16),
            pltpu.VMEM((LINES, OBS), F32),
            pltpu.VMEM((LINES, OBS), F32),
            pltpu.VMEM((LINES, OBS), BF16),
            pltpu.VMEM((LINES, OBS), BF16),
            pltpu.VMEM((2 * GROUPS * EDGE, OBS), F32),
            pltpu.VMEM((2 * GROUPS * EDGE, OBS), BF16),
            pltpu.VMEM((2 * C, NY), BF16),
            pltpu.VMEM((NY, C), BF16),
            pltpu.VMEM((2 * LINES, NY), BF16),
            pltpu.VMEM((2 * LINES, NY), BF16),
            edge,
            edge,
            edge,
            edge,
            pltpu.VMEM((4, OBS), F32),
            pltpu.VMEM((YS - 1, 4, OBS), F32),
            pltpu.VMEM((4, OBS), F32),
            pltpu.VMEM((2, 4, OBS), F32),
            pltpu.VMEM((4, OBS), F32),
            pltpu.VMEM((4 * LINES, OBS), BF16),
            pltpu.VMEM((2 * LINES, OBS), BF16),
            edge,
            edge,
            edge,
            edge,
            pltpu.VMEM((2, LINES, NY), F32),
            rows3,
            rows3,
            rows3,
            rows3,
            pltpu.SemaphoreType.DMA((2,)),
            pltpu.SemaphoreType.DMA((4 * CHUNKS + 4 * GROUPS + YS + 3,)),
            pltpu.SemaphoreType.DMA((4 * CHUNKS + 4 * GROUPS + YS + 3,)),
        ],
        compiler_params=pltpu.CompilerParams(
            collective_id=0, has_side_effects=True, vmem_limit_bytes=56 * 1024 * 1024
        ),
    )(
        alpha.reshape(M * L * R, C),
        perturbation,
        obs_cell.reshape(row),
        obs_kind.reshape(row),
        obs_value.reshape(row),
        obs_weight.reshape(row),
    )
    return (out + rest).reshape(M, L, R, C)


def solution(mesh):
    regions, groups = mesh.shape["reg"], mesh.shape["mem"]
    return jax.shard_map(
        functools.partial(local, regions, M * groups),
        mesh=mesh,
        in_specs=(
            P("mem", None, "reg", None),
            P("mem", None, None, "reg", None),
            P("reg"),
            P("reg"),
            P("reg"),
            P("reg"),
        ),
        out_specs=P("mem", None, "reg", None),
        check_vma=False,
    )
```

```python
import functools
import math

import jax
import jax.numpy as jnp
from jax import lax
from jax.experimental import pallas as pl
from jax.experimental.pallas import tpu as pltpu
from jax.sharding import PartitionSpec as P

MESH = pl.DeviceIdType.MESH
F32, BF16, I32 = jnp.float32, jnp.bfloat16, jnp.int32
diffuse = 0.2

YS = 4
ZS = 4
M, L, R, C = 8, 16, 4, 128
RX, NY, OBS = 16, 512, 1024
LINES = L * RX
LB = 2
CHUNKS = L // LB
ROWS = LB * M
GROUPS = 4
PER = CHUNKS // GROUPS
EDGE = 2 * (L // GROUPS)
NT = (((1,), (1,)), ((), ()))


def split(value):
    high = value.astype(BF16)
    return high, (value - high.astype(F32)).astype(BF16)


def dot(a, b):
    return jnp.dot(a, b, preferred_element_type=F32)


def dot_nt(a, b):
    return lax.dot_general(a, b, NT, preferred_element_type=F32)


def sides(value):
    lane = lax.broadcasted_iota(I32, value.shape, 1)
    left = jnp.where(lane == 0, 0.0, pltpu.roll(value, 1, 1))
    right = jnp.where(lane == C - 1, 0.0, pltpu.roll(value, C - 1, 1))
    return left + right


def one_pass(rows, first, last, inside):
    out = {}
    for k in range(first, last + 1):
        here, above, below = rows.get(k), rows.get(k - 1), rows.get(k + 1)
        vertical = [v for v in (above, below) if v is not None]
        beside = vertical[0] if len(vertical) == 1 else vertical[0] + vertical[1] if vertical else None
        if here is not None:
            beside = sides(here) if beside is None else beside + sides(here)
            value = here + diffuse * (beside - 4.0 * here)
        else:
            value = diffuse * beside
        out[k] = inside(k, value)
    return out


def kernel(
    scale,
    regions,
    alpha_hbm,
    pert_hbm,
    cell_ref,
    kind_ref,
    val_ref,
    wt_ref,
    out_ref,
    rest_ref,
    pert,
    alpha,
    slab,
    part,
    c0t,
    c1t,
    r0f,
    r1f,
    r0b,
    r1b,
    rimf,
    rimb,
    py2,
    pyt,
    fields,
    etop,
    ebot,
    rtop,
    rbot,
    streams,
    lc,
    lh,
    ftop,
    fbot,
    gtop,
    gbot,
    grad,
    sup,
    sdn,
    qup,
    qdn,
    local_sem,
    send_sem,
    recv_sem,
):
    mem = lax.axis_index("mem")
    reg = lax.axis_index("reg")
    y, zh = lax.rem(mem, YS), mem // YS
    up = lax.rem(reg + 1, regions)
    down = lax.rem(reg + regions - 1, regions)
    has_prev = reg > 0
    has_next = reg < regions - 1
    y_peers = [zh * YS + lax.rem(y + d, YS) for d in range(1, YS)]
    z_up = lax.rem(zh + 1, ZS) * YS + y
    z_down = lax.rem(zh + ZS - 1, ZS) * YS + y

    def remote(source, target, index, **where):
        return pltpu.make_async_remote_copy(
            src_ref=source,
            dst_ref=target,
            send_sem=send_sem.at[index],
            recv_sem=recv_sem.at[index],
            device_id=where,
            device_id_type=MESH,
        )

    def send(*args, **where):
        copy = remote(*args, **where)
        copy.start()
        return copy

    def rims_in(c):
        at = pl.ds(pl.multiple_of(c * ROWS, ROWS), ROWS)
        return (
            remote(slab.at[pl.ds(4, 3), at], slab.at[pl.ds(0, 3), at], c, reg=up),
            remote(slab.at[pl.ds(3, 3), at], slab.at[pl.ds(7, 3), at], CHUNKS + c, reg=down),
        )

    def rims_out(c):
        at = pl.ds(pl.multiple_of(c * ROWS, ROWS), ROWS)
        first = 2 * CHUNKS
        return (
            remote(sdn.at[:, at], qdn.at[:, at], first + c, reg=down),
            remote(sup.at[:, at], qup.at[:, at], first + CHUNKS + c, reg=up),
        )

    def edges(g):
        first = 4 * CHUNKS
        return (
            remote(etop.at[g], rbot.at[g], first + g, reg=down),
            remote(ebot.at[g], rtop.at[g], first + GROUPS + g, reg=up),
        )

    def edges_back(g):
        first = 4 * CHUNKS + 2 * GROUPS
        return (
            remote(ftop.at[g], gbot.at[g], first + g, reg=down),
            remote(fbot.at[g], gtop.at[g], first + GROUPS + g, reg=up),
        )

    winds, acrosses, alongs = streams
    sums = 4 * CHUNKS + 4 * GROUPS

    def y_copies(n):
        mine, from_y = streams[n][0], streams[n][1]
        return [
            remote(mine, from_y.at[d], sums + 6 * n + d, mem=who) for d, who in enumerate(y_peers)
        ]

    def near(n, turn):
        held, from_z = streams[n][2], streams[n][3]
        side = turn if n == 0 else 1 - turn
        where = (z_up, z_down)[side]
        return remote(held, from_z.at[side], sums + 6 * n + 3 + side, mem=where)

    def far(n):
        from_z, from_far = streams[n][3], streams[n][4]
        where, side = (z_up, 0) if n == 0 else (z_down, 1)
        return remote(from_z.at[side], from_far, sums + 6 * n + 5, mem=where)

    def y_start(n):
        begin(y_copies(n))

    def y_end(n):
        mine, from_y, held = streams[n][:3]
        finish(y_copies(n))
        total = mine[...]
        for d in range(YS - 1):
            total = total + from_y[d]
        held[...] = total
        begin((near(n, 0), near(n, 1)))

    def z_middle(n):
        near(n, 0).wait()
        far(n).start()

    def z_end(n):
        held, from_z, from_far = streams[n][2:]
        near(n, 1).wait()
        far(n).wait()
        return held[...] + from_z[0] + from_z[1] + from_far[...]

    def begin(copies):
        for copy in copies:
            copy.start()

    def finish(copies):
        for copy in copies:
            copy.wait()

    def each(count, body):
        def step(i, _):
            body(i)
            return _

        lax.fori_loop(0, count, step, 0)

    barrier = pltpu.get_barrier_semaphore()
    for who in (up, down):
        pl.semaphore_signal(barrier, inc=1, device_id={"reg": who}, device_id_type=MESH)
    for who in y_peers + [z_up, z_down]:
        pl.semaphore_signal(barrier, inc=1, device_id={"mem": who}, device_id_type=MESH)
    def get_alpha(c):
        at = pl.ds(pl.multiple_of(c * (LB * R), LB * R), LB * R)
        return pltpu.make_async_copy(alpha_hbm.at[:, at], alpha.at[:, at], local_sem.at[1 + c])

    each(CHUNKS, lambda c: get_alpha(c).start())
    get_pert = pltpu.make_async_copy(pert_hbm, pert, local_sem.at[0])
    get_pert.start()
    pl.semaphore_wait(barrier, 2 + YS - 1 + 2)
    flat = alpha.reshape(M * L * R, C)

    def arrange(c):
        get_alpha(c).wait()
        for k in range(LB):
            lev = c * LB + k
            at = pl.multiple_of(lev * M, M)
            for r in range(R):
                slab[3 + r, pl.ds(at, M), :] = flat[pl.ds(lev * R + r, M, stride=L * R), :]
        begin(rims_in(c))

    each(CHUNKS, arrange)

    cell = cell_ref[...]
    kind = kind_ref[...]
    column = cell & (NY - 1)
    row_in = (cell >> 9) & (RX - 1)
    level = cell >> 13
    line = cell >> 9
    line_m = jnp.where(row_in > 0, line - 1, -1)
    line_p = jnp.where(row_in < RX - 1, line + 1, -1)
    per = L // GROUPS
    place = (level // per) * EDGE + level % per + jnp.where(kind == 2, per, 0)
    place = jnp.where(row_in == 0, place, GROUPS * EDGE + place)
    place = jnp.where((kind >= 2) & ((row_in == 0) | (row_in == RX - 1)), place, -1)
    number = lax.broadcasted_iota(I32, (2 * GROUPS * EDGE, OBS), 0)
    outer = jnp.where(number == place, jnp.where(row_in == 0, -0.5, 0.5), 0.0)
    rimf[...] = outer
    rimb[...] = outer.astype(BF16)

    def build_columns(step, _):
        at = pl.multiple_of(step * 32, 32)
        number = lax.broadcasted_iota(I32, (32, OBS), 0) + at
        c0t[pl.ds(at, 32), :] = jnp.where(number == column, 1.0, 0.0).astype(BF16)
        c1t[pl.ds(at, 32), :] = jnp.where(
            number == column + 1, 0.5, jnp.where(number == column - 1, -0.5, 0.0)
        ).astype(BF16)
        return _

    lax.fori_loop(0, NY // 32, build_columns, 0)

    def build_lines(step, _):
        at = pl.multiple_of(step * 32, 32)
        number = lax.broadcasted_iota(I32, (32, OBS), 0) + at
        r0 = jnp.where(number == line, 1.0, 0.0)
        r1 = jnp.where(number == line_p, 0.5, jnp.where(number == line_m, -0.5, 0.0))
        r0f[pl.ds(at, 32), :] = r0
        r1f[pl.ds(at, 32), :] = r1
        r0b[pl.ds(at, 32), :] = r0.astype(BF16)
        r1b[pl.ds(at, 32), :] = r1.astype(BF16)
        return _

    lax.fori_loop(0, LINES // 32, build_lines, 0)

    def table(shape, fine_dim):
        fine = lax.broadcasted_iota(I32, shape, fine_dim).astype(F32)
        coarse = lax.broadcasted_iota(I32, shape, 1 - fine_dim).astype(F32)
        return jnp.maximum(0.0, 1.0 - jnp.abs((fine + 0.5) / 4.0 - 0.5 - coarse)).astype(BF16)

    weights = table((C, NY), 1)
    py2[0:C, :] = weights
    py2[C : 2 * C, :] = weights
    pyt[...] = table((NY, C), 0)

    def inside(k, value):
        if k < 0:
            return jnp.where(has_prev, value, 0.0)
        if k >= R:
            return jnp.where(has_next, value, 0.0)
        return value

    get_pert.wait()

    def increments(group):
        for h in range(PER):
            c = group * PER + h
            finish(rims_in(c))
            at = pl.multiple_of(c * ROWS, ROWS)
            rows = {k - 3: inside(k - 3, slab[k, pl.ds(at, ROWS), :]) for k in range(R + 6)}
            rows = one_pass(rows, -2, R + 1, inside)
            rows = one_pass(rows, -1, R, inside)
            at = pl.multiple_of(c * (ROWS * RX), ROWS * RX)
            for i in range(RX):
                q, s = divmod(i, 4)
                mine, other = ((0.625, 0.375), (0.875, 0.125), (0.875, 0.125), (0.625, 0.375))[s]
                near = q - 1 if s < 2 else q + 1
                part[pl.ds(at + i, ROWS, stride=RX), :] = mine * rows[q] + other * rows[near]
            high, low = split(part[pl.ds(at, ROWS * RX), :])
            fine = dot(jnp.concatenate([high, low], axis=1), py2[...])
            for k in range(LB):
                lev = c * LB + k
                for w in range(2):
                    total = None
                    for m in range(M):
                        at = (k * M + m) * RX
                        term = fine[at : at + RX] * pert[m, w, lev].astype(F32)
                        total = term if total is None else total + term
                    at = pl.multiple_of(lev * RX, RX)
                    fields[2 * w, pl.ds(at, RX), :], fields[2 * w + 1, pl.ds(at, RX), :] = split(total)
                    row = w * (EDGE // 2) + h * LB + k
                    etop[group, row : row + 1, :] = total[0:1]
                    ebot[group, row : row + 1, :] = total[RX - 1 : RX]
        begin(edges(group))

    each(GROUPS, increments)

    NB = 256

    def pick(step, _):
        at = pl.multiple_of(step * NB, NB)
        at = pl.ds(at, NB)
        second = kind_ref[:, at] == 2
        on, beside = r0f[:, at], r1f[:, at]

        def over(lines):
            return jnp.sum(lines, axis=0, keepdims=True)

        value = dot(fields[...].reshape(4 * LINES, NY), c0t[:, at])
        at_u = value[0:LINES] + value[LINES : 2 * LINES]
        at_v = value[2 * LINES : 3 * LINES] + value[3 * LINES :]
        winds[0][0:1, at] = over(on * at_u)
        winds[0][1:2, at] = over(on * at_v)
        alongs[0][:, at] = over(beside * jnp.where(second, at_v, at_u))
        value = dot(fields[0:2].reshape(2 * LINES, NY), c1t[:, at])
        acrosses[0][:, at] = over(on * (value[0:LINES] + value[LINES:]))
        return _

    lax.fori_loop(0, OBS // NB, pick, 0)
    y_start(0)
    y_start(1)
    each(GROUPS, lambda g: finish(edges(g)))
    sides_in = [
        jnp.where(has_prev, rtop[...].reshape(GROUPS * EDGE, NY), 0.0),
        jnp.where(has_next, rbot[...].reshape(GROUPS * EDGE, NY), 0.0),
    ]
    high, low = split(jnp.concatenate(sides_in, axis=0))
    rim = dot(high, c0t[...]) + dot(low, c0t[...])
    alongs[0][...] = alongs[0][...] + jnp.sum(rimf[...] * rim, axis=0, keepdims=True)
    y_start(2)

    for n in range(3):
        y_end(n)
    for n in range(3):
        z_middle(n)
    (both, slope_y, slope_x) = (z_end(n) * scale for n in range(3))
    u, v = both[0:1], both[1:2]
    is_u, is_v, is_vort, is_adv = kind == 0, kind == 1, kind == 2, kind == 3
    seen = jnp.where(
        is_u,
        u,
        jnp.where(is_v, v, jnp.where(is_vort, slope_x - slope_y, u * slope_x + v * slope_y)),
    )
    misfit = wt_ref[...] * (seen - val_ref[...]) * scale
    zero = jnp.zeros_like(misfit)
    to_u = split(jnp.where(is_u, misfit, jnp.where(is_adv, misfit * slope_x, zero)))
    to_v = split(jnp.where(is_v, misfit, jnp.where(is_adv, misfit * slope_y, zero)))
    along_u = split(jnp.where(is_adv, misfit * u, zero))
    along_v = split(jnp.where(is_vort, misfit, zero))
    across = split(jnp.where(is_vort, -misfit, jnp.where(is_adv, misfit * v, zero)))

    high = rimb[...] * (along_u[0] + along_v[0])
    low = rimb[...] * (along_u[1] + along_v[1])
    rim = dot_nt(high, c0t[...]) + dot_nt(low, c0t[...])
    ftop[...] = rim[: GROUPS * EDGE].reshape(GROUPS, EDGE, NY)
    fbot[...] = rim[GROUPS * EDGE :].reshape(GROUPS, EDGE, NY)
    each(GROUPS, lambda g: begin(edges_back(g)))

    for half in range(2):
        lc[half * LINES : (half + 1) * LINES, :] = (
            r0b[0:LINES, :] * to_u[half] + r1b[0:LINES, :] * along_u[half]
        )
        lc[(2 + half) * LINES : (3 + half) * LINES, :] = (
            r0b[0:LINES, :] * to_v[half] + r1b[0:LINES, :] * along_v[half]
        )
        lh[half * LINES : (half + 1) * LINES, :] = r0b[0:LINES, :] * across[half]

    def scatter(step, _):
        at = pl.multiple_of(step * NB, NB)
        value = dot_nt(lc[...], c0t[pl.ds(at, NB), :])
        slope = dot_nt(lh[...], c1t[pl.ds(at, NB), :])
        grad[0, :, pl.ds(at, NB)] = (value[0:LINES] + value[LINES : 2 * LINES]) + (
            slope[0:LINES] + slope[LINES:]
        )
        grad[1, :, pl.ds(at, NB)] = value[2 * LINES : 3 * LINES] + value[3 * LINES :]
        return _

    lax.fori_loop(0, NY // NB, scatter, 0)

    def project(group):
        finish(edges_back(group))
        for h in range(PER):
            c = group * PER + h
            pieces = []
            row = lax.broadcasted_iota(I32, (RX, NY), 0)
            for k in range(LB):
                lev = c * LB + k
                at = pl.multiple_of(lev * RX, RX)
                gradients = []
                for w in range(2):
                    edge = w * (EDGE // 2) + h * LB + k
                    first = jnp.where(has_prev, gtop[group, edge : edge + 1, :], 0.0)
                    last = jnp.where(has_next, gbot[group, edge : edge + 1, :], 0.0)
                    gradients.append(
                        grad[w, pl.ds(at, RX), :]
                        + jnp.where(row == 0, first, jnp.where(row == RX - 1, last, 0.0))
                    )
                for m in range(M):
                    pieces.append(
                        gradients[0] * pert[m, 0, lev].astype(F32)
                        + gradients[1] * pert[m, 1, lev].astype(F32)
                    )
            high, low = split(jnp.concatenate(pieces, axis=0))
            at = pl.multiple_of(c * (ROWS * RX), ROWS * RX)
            value = dot(jnp.concatenate([high, low], axis=0), pyt[...])
            part[pl.ds(at, ROWS * RX), :] = value[: ROWS * RX] + value[ROWS * RX :]
            f = [part[pl.ds(at + i, ROWS, stride=RX), :] for i in range(RX)]
            taps = (0.125, 0.375, 0.625, 0.875, 0.875, 0.625, 0.375, 0.125)
            rows = {}
            for q in range(-1, R + 1):
                value = None
                for t, tap in enumerate(taps):
                    i = 4 * q - 2 + t
                    if 0 <= i < RX:
                        term = tap * f[i]
                        value = term if value is None else value + term
                rows[q] = inside(q, value)
            rows = one_pass(rows, -2, R + 1, inside)
            rows = one_pass(rows, -3, R + 2, inside)
            at = pl.multiple_of(c * ROWS, ROWS)
            for k in range(3):
                sdn[k, pl.ds(at, ROWS), :] = rows[k - 3]
                sup[k, pl.ds(at, ROWS), :] = rows[R + k]
            for k in range(LB):
                for r in range(R):
                    out_ref[pl.ds((c * LB + k) * R + r, M, stride=L * R), :] = rows[r][
                        k * M : (k + 1) * M
                    ]
            begin(rims_out(c))

    each(GROUPS, project)

    def collect(c):
        finish(rims_out(c))
        for k in range(LB):
            at = pl.multiple_of(c * ROWS + k * M, M)
            for r in range(R):
                value = 0.0
                if r < 3:
                    value = value + jnp.where(has_prev, qup[r, pl.ds(at, M), :], 0.0)
                if r >= R - 3:
                    value = value + jnp.where(has_next, qdn[r - (R - 3), pl.ds(at, M), :], 0.0)
                rest_ref[pl.ds((c * LB + k) * R + r, M, stride=L * R), :] = value

    each(CHUNKS, collect)


def local(regions, members, alpha, perturbation, obs_cell, obs_kind, obs_value, obs_weight):
    any_space = pl.BlockSpec(memory_space=pl.ANY)
    in_vmem = pl.BlockSpec(memory_space=pltpu.VMEM)
    row = (1, OBS)
    edge = pltpu.VMEM((GROUPS, EDGE, NY), F32)
    rows3 = pltpu.VMEM((3, M * L, C), F32)

    def stream(rows):
        one = pltpu.VMEM((rows, OBS), F32)
        return (
            one,
            pltpu.VMEM((YS - 1, rows, OBS), F32),
            one,
            pltpu.VMEM((2, rows, OBS), F32),
            one,
        )

    out, rest = pl.pallas_call(
        functools.partial(kernel, 1.0 / math.sqrt(members), regions),
        out_shape=[jax.ShapeDtypeStruct((M * L * R, C), F32)] * 2,
        in_specs=[any_space, any_space] + [in_vmem] * 4,
        out_specs=[in_vmem] * 2,
        scratch_shapes=[
            pltpu.VMEM((M, 2, L, RX, NY), BF16),
            pltpu.VMEM((M, L * R, C), F32),
            pltpu.VMEM((R + 6, M * L, C), F32),
            pltpu.VMEM((M * L * RX, C), F32),
            pltpu.VMEM((NY, OBS), BF16),
            pltpu.VMEM((NY, OBS), BF16),
            pltpu.VMEM((LINES, OBS), F32),
            pltpu.VMEM((LINES, OBS), F32),
            pltpu.VMEM((LINES, OBS), BF16),
            pltpu.VMEM((LINES, OBS), BF16),
            pltpu.VMEM((2 * GROUPS * EDGE, OBS), F32),
            pltpu.VMEM((2 * GROUPS * EDGE, OBS), BF16),
            pltpu.VMEM((2 * C, NY), BF16),
            pltpu.VMEM((NY, C), BF16),
            pltpu.VMEM((4, LINES, NY), BF16),
            edge,
            edge,
            edge,
            edge,
            tuple(stream(rows) for rows in (2, 1, 1)),
            pltpu.VMEM((4 * LINES, OBS), BF16),
            pltpu.VMEM((2 * LINES, OBS), BF16),
            edge,
            edge,
            edge,
            edge,
            pltpu.VMEM((2, LINES, NY), F32),
            rows3,
            rows3,
            rows3,
            rows3,
            pltpu.SemaphoreType.DMA((1 + CHUNKS,)),
            pltpu.SemaphoreType.DMA((4 * CHUNKS + 4 * GROUPS + 18,)),
            pltpu.SemaphoreType.DMA((4 * CHUNKS + 4 * GROUPS + 18,)),
        ],
        compiler_params=pltpu.CompilerParams(
            collective_id=0, has_side_effects=True, vmem_limit_bytes=56 * 1024 * 1024
        ),
    )(
        alpha.reshape(M, L * R, C),
        perturbation,
        obs_cell.reshape(row),
        obs_kind.reshape(row),
        obs_value.reshape(row),
        obs_weight.reshape(row),
    )
    return (out + rest).reshape(M, L, R, C)


def solution(mesh):
    regions, groups = mesh.shape["reg"], mesh.shape["mem"]
    return jax.shard_map(
        functools.partial(local, regions, M * groups),
        mesh=mesh,
        in_specs=(
            P("mem", None, "reg", None),
            P("mem", None, None, "reg", None),
            P("reg"),
            P("reg"),
            P("reg"),
            P("reg"),
        ),
        out_specs=P("mem", None, "reg", None),
        check_vma=False,
    )
```

```python
import functools
import math

import jax
import jax.numpy as jnp
from jax import lax
from jax.experimental import pallas as pl
from jax.experimental.pallas import tpu as pltpu
from jax.sharding import PartitionSpec as P

MESH = pl.DeviceIdType.MESH
F32, BF16, I32 = jnp.float32, jnp.bfloat16, jnp.int32
diffuse = 0.2

YS = 4
ZS = 4
M, L, R, C = 8, 16, 4, 128
RX, NY, OBS = 16, 512, 1024
LINES = L * RX
LB = 2
CHUNKS = L // LB
ROWS = LB * M
GROUPS = 4
PER = CHUNKS // GROUPS
EDGE = 2 * (L // GROUPS)
NT = (((1,), (1,)), ((), ()))


def split(value):
    high = value.astype(BF16)
    return high, (value - high.astype(F32)).astype(BF16)


def dot(a, b):
    return jnp.dot(a, b, preferred_element_type=F32)


def dot_nt(a, b):
    return lax.dot_general(a, b, NT, preferred_element_type=F32)


def sides(value):
    lane = lax.broadcasted_iota(I32, value.shape, 1)
    left = jnp.where(lane == 0, 0.0, pltpu.roll(value, 1, 1))
    right = jnp.where(lane == C - 1, 0.0, pltpu.roll(value, C - 1, 1))
    return left + right


def one_pass(rows, first, last, inside):
    out = {}
    for k in range(first, last + 1):
        value = None
        for near in (k - 1, k, k + 1):
            if near in rows:
                value = rows[near] if value is None else value + rows[near]
        if k in rows:
            value = value + sides(rows[k])
        out[k] = inside(k, value)
    return out


def kernel(
    scale,
    regions,
    alpha_hbm,
    pert_hbm,
    cell_ref,
    kind_ref,
    val_ref,
    wt_ref,
    out_ref,
    rest_ref,
    pert,
    alpha,
    slab,
    part,
    c0t,
    c1t,
    r0f,
    r1f,
    r0b,
    r1b,
    rimf,
    rimb,
    py2,
    pyt,
    fields,
    etop,
    ebot,
    rtop,
    rbot,
    streams,
    lc,
    lh,
    ftop,
    fbot,
    gtop,
    gbot,
    grad,
    sup,
    sdn,
    qup,
    qdn,
    local_sem,
    send_sem,
    recv_sem,
):
    mem = lax.axis_index("mem")
    reg = lax.axis_index("reg")
    y, zh = lax.rem(mem, YS), mem // YS
    up = lax.rem(reg + 1, regions)
    down = lax.rem(reg + regions - 1, regions)
    has_prev = reg > 0
    has_next = reg < regions - 1
    y_peers = [zh * YS + lax.rem(y + d, YS) for d in range(1, YS)]
    z_peers = [lax.rem(zh + d, ZS) * YS + y for d in range(1, ZS)]

    def remote(source, target, index, **where):
        return pltpu.make_async_remote_copy(
            src_ref=source,
            dst_ref=target,
            send_sem=send_sem.at[index],
            recv_sem=recv_sem.at[index],
            device_id=where,
            device_id_type=MESH,
        )

    def send(*args, **where):
        copy = remote(*args, **where)
        copy.start()
        return copy

    def rims_in(c):
        at = pl.ds(pl.multiple_of(c * ROWS, ROWS), ROWS)
        return (
            remote(slab.at[pl.ds(4, 3), at], slab.at[pl.ds(0, 3), at], c, reg=up),
            remote(slab.at[pl.ds(3, 3), at], slab.at[pl.ds(7, 3), at], CHUNKS + c, reg=down),
        )

    def rims_out(c):
        at = pl.ds(pl.multiple_of(c * ROWS, ROWS), ROWS)
        first = 2 * CHUNKS
        return (
            remote(sdn.at[:, at], qdn.at[:, at], first + c, reg=down),
            remote(sup.at[:, at], qup.at[:, at], first + CHUNKS + c, reg=up),
        )

    def edges(g):
        first = 4 * CHUNKS
        return (
            remote(etop.at[g], rbot.at[g], first + g, reg=down),
            remote(ebot.at[g], rtop.at[g], first + GROUPS + g, reg=up),
        )

    def edges_back(g):
        first = 4 * CHUNKS + 2 * GROUPS
        return (
            remote(ftop.at[g], gbot.at[g], first + g, reg=down),
            remote(fbot.at[g], gtop.at[g], first + GROUPS + g, reg=up),
        )

    fields_out, along_out = streams[0][0], streams[1][0]
    sums = 4 * CHUNKS + 4 * GROUPS

    def y_copies(n):
        mine, from_y = streams[n][0], streams[n][1]
        return [
            remote(mine, from_y.at[d], sums + 6 * n + d, mem=who) for d, who in enumerate(y_peers)
        ]

    def z_copies(n):
        held, from_z = streams[n][2], streams[n][3]
        return [
            remote(held, from_z.at[d], sums + 6 * n + 3 + d, mem=who)
            for d, who in reversed(list(enumerate(z_peers)))
        ]

    def y_start(n):
        begin(y_copies(n))

    def y_end(n):
        mine, from_y, held = streams[n][:3]
        finish(y_copies(n))
        total = mine[...]
        for d in range(YS - 1):
            total = total + from_y[d]
        held[...] = total
        begin(z_copies(n))

    def z_end(n):
        held, from_z = streams[n][2:]
        finish(z_copies(n))
        total = held[...]
        for d in range(ZS - 1):
            total = total + from_z[d]
        return total

    def begin(copies):
        for copy in copies:
            copy.start()

    def finish(copies):
        for copy in copies:
            copy.wait()

    def each(count, body):
        def step(i, _):
            body(i)
            return _

        lax.fori_loop(0, count, step, 0)

    barrier = pltpu.get_barrier_semaphore()
    for who in (up, down):
        pl.semaphore_signal(barrier, inc=1, device_id={"reg": who}, device_id_type=MESH)
    for who in y_peers + z_peers:
        pl.semaphore_signal(barrier, inc=1, device_id={"mem": who}, device_id_type=MESH)
    def get_alpha(c):
        at = pl.ds(pl.multiple_of(c * (LB * R), LB * R), LB * R)
        return pltpu.make_async_copy(alpha_hbm.at[:, at], alpha.at[:, at], local_sem.at[1 + c])

    each(CHUNKS, lambda c: get_alpha(c).start())
    get_pert = pltpu.make_async_copy(pert_hbm, pert, local_sem.at[0])
    get_pert.start()
    pl.semaphore_wait(barrier, 2 + YS - 1 + ZS - 1)
    flat = alpha.reshape(M * L * R, C)

    def arrange(c):
        get_alpha(c).wait()
        for k in range(LB):
            lev = c * LB + k
            at = pl.multiple_of(lev * M, M)
            for r in range(R):
                slab[3 + r, pl.ds(at, M), :] = flat[pl.ds(lev * R + r, M, stride=L * R), :]
        begin(rims_in(c))

    each(CHUNKS, arrange)

    cell = cell_ref[...]
    kind = kind_ref[...]
    column = cell & (NY - 1)
    row_in = (cell >> 9) & (RX - 1)
    level = cell >> 13
    line = cell >> 9
    line_m = jnp.where(row_in > 0, line - 1, -1)
    line_p = jnp.where(row_in < RX - 1, line + 1, -1)
    per = L // GROUPS
    place = (level // per) * EDGE + level % per + jnp.where(kind == 2, per, 0)
    place = jnp.where(row_in == 0, place, GROUPS * EDGE + place)
    place = jnp.where((kind >= 2) & ((row_in == 0) | (row_in == RX - 1)), place, -1)
    number = lax.broadcasted_iota(I32, (2 * GROUPS * EDGE, OBS), 0)
    outer = jnp.where(number == place, jnp.where(row_in == 0, -0.5, 0.5), 0.0)
    rimf[...] = outer
    rimb[...] = outer.astype(BF16)

    def build_columns(step, _):
        at = pl.multiple_of(step * 32, 32)
        number = lax.broadcasted_iota(I32, (32, OBS), 0) + at
        c0t[pl.ds(at, 32), :] = jnp.where(number == column, 1.0, 0.0).astype(BF16)
        c1t[pl.ds(at, 32), :] = jnp.where(
            number == column + 1, 0.5, jnp.where(number == column - 1, -0.5, 0.0)
        ).astype(BF16)
        return _

    lax.fori_loop(0, NY // 32, build_columns, 0)

    def build_lines(step, _):
        at = pl.multiple_of(step * 32, 32)
        number = lax.broadcasted_iota(I32, (32, OBS), 0) + at
        r0 = jnp.where(number == line, 1.0, 0.0)
        r1 = jnp.where(number == line_p, 0.5, jnp.where(number == line_m, -0.5, 0.0))
        r0f[pl.ds(at, 32), :] = r0
        r1f[pl.ds(at, 32), :] = r1
        r0b[pl.ds(at, 32), :] = r0.astype(BF16)
        r1b[pl.ds(at, 32), :] = r1.astype(BF16)
        return _

    lax.fori_loop(0, LINES // 32, build_lines, 0)

    def table(shape, fine_dim):
        fine = lax.broadcasted_iota(I32, shape, fine_dim).astype(F32)
        coarse = lax.broadcasted_iota(I32, shape, 1 - fine_dim).astype(F32)
        return jnp.maximum(0.0, 1.0 - jnp.abs((fine + 0.5) / 4.0 - 0.5 - coarse)).astype(BF16)

    weights = table((C, NY), 1)
    py2[0:C, :] = weights
    py2[C : 2 * C, :] = weights
    pyt[...] = table((NY, C), 0)

    def inside(k, value):
        if k < 0:
            return jnp.where(has_prev, value, 0.0)
        if k >= R:
            return jnp.where(has_next, value, 0.0)
        return value

    get_pert.wait()

    def increments(group):
        for h in range(PER):
            c = group * PER + h
            finish(rims_in(c))
            at = pl.multiple_of(c * ROWS, ROWS)
            rows = {k - 3: inside(k - 3, slab[k, pl.ds(at, ROWS), :]) for k in range(R + 6)}
            rows = one_pass(rows, -2, R + 1, inside)
            rows = one_pass(rows, -1, R, inside)
            at = pl.multiple_of(c * (ROWS * RX), ROWS * RX)
            for i in range(RX):
                q, s = divmod(i, 4)
                mine, other = ((0.625, 0.375), (0.875, 0.125), (0.875, 0.125), (0.625, 0.375))[s]
                near = q - 1 if s < 2 else q + 1
                part[pl.ds(at + i, ROWS, stride=RX), :] = (diffuse * diffuse * mine) * rows[q] + (
                    diffuse * diffuse * other
                ) * rows[near]
            high, low = split(part[pl.ds(at, ROWS * RX), :])
            fine = dot(jnp.concatenate([high, low], axis=1), py2[...])
            for k in range(LB):
                lev = c * LB + k
                for w in range(2):
                    total = None
                    for m in range(M):
                        at = (k * M + m) * RX
                        term = fine[at : at + RX] * pert[m, w, lev].astype(F32)
                        total = term if total is None else total + term
                    at = pl.multiple_of(lev * RX, RX)
                    fields[2 * w, pl.ds(at, RX), :], fields[2 * w + 1, pl.ds(at, RX), :] = split(total)
                    row = w * (EDGE // 2) + h * LB + k
                    etop[group, row : row + 1, :] = total[0:1]
                    ebot[group, row : row + 1, :] = total[RX - 1 : RX]
        begin(edges(group))

    each(GROUPS, increments)

    NB = 256

    def pick(step, _):
        at = pl.multiple_of(step * NB, NB)
        at = pl.ds(at, NB)
        second = kind_ref[:, at] == 2
        on, beside = r0f[:, at], r1f[:, at]

        def over(lines):
            return jnp.sum(lines, axis=0, keepdims=True)

        value = dot(fields[...].reshape(4 * LINES, NY), c0t[:, at])
        at_u = value[0:LINES] + value[LINES : 2 * LINES]
        at_v = value[2 * LINES : 3 * LINES] + value[3 * LINES :]
        fields_out[0:1, at] = over(on * at_u)
        fields_out[1:2, at] = over(on * at_v)
        along_out[:, at] = over(beside * jnp.where(second, at_v, at_u))
        value = dot(fields[0:2].reshape(2 * LINES, NY), c1t[:, at])
        fields_out[2:3, at] = over(on * (value[0:LINES] + value[LINES:]))
        return _

    lax.fori_loop(0, OBS // NB, pick, 0)
    y_start(0)
    each(GROUPS, lambda g: finish(edges(g)))
    sides_in = [
        jnp.where(has_prev, rtop[...].reshape(GROUPS * EDGE, NY), 0.0),
        jnp.where(has_next, rbot[...].reshape(GROUPS * EDGE, NY), 0.0),
    ]
    high, low = split(jnp.concatenate(sides_in, axis=0))
    rim = dot(high, c0t[...]) + dot(low, c0t[...])
    along_out[...] = along_out[...] + jnp.sum(rimf[...] * rim, axis=0, keepdims=True)
    y_start(1)

    y_end(0)
    y_end(1)
    total, slope_x = z_end(0) * scale, z_end(1) * scale
    u, v, slope_y = total[0:1], total[1:2], total[2:3]
    is_u, is_v, is_vort, is_adv = kind == 0, kind == 1, kind == 2, kind == 3
    seen = jnp.where(
        is_u,
        u,
        jnp.where(is_v, v, jnp.where(is_vort, slope_x - slope_y, u * slope_x + v * slope_y)),
    )
    misfit = wt_ref[...] * (seen - val_ref[...]) * scale
    zero = jnp.zeros_like(misfit)
    to_u = split(jnp.where(is_u, misfit, jnp.where(is_adv, misfit * slope_x, zero)))
    to_v = split(jnp.where(is_v, misfit, jnp.where(is_adv, misfit * slope_y, zero)))
    along_u = split(jnp.where(is_adv, misfit * u, zero))
    along_v = split(jnp.where(is_vort, misfit, zero))
    across = split(jnp.where(is_vort, -misfit, jnp.where(is_adv, misfit * v, zero)))

    high = rimb[...] * (along_u[0] + along_v[0])
    low = rimb[...] * (along_u[1] + along_v[1])
    rim = dot_nt(high, c0t[...]) + dot_nt(low, c0t[...])
    ftop[...] = rim[: GROUPS * EDGE].reshape(GROUPS, EDGE, NY)
    fbot[...] = rim[GROUPS * EDGE :].reshape(GROUPS, EDGE, NY)
    each(GROUPS, lambda g: begin(edges_back(g)))

    for half in range(2):
        lc[half * LINES : (half + 1) * LINES, :] = (
            r0b[0:LINES, :] * to_u[half] + r1b[0:LINES, :] * along_u[half]
        )
        lc[(2 + half) * LINES : (3 + half) * LINES, :] = (
            r0b[0:LINES, :] * to_v[half] + r1b[0:LINES, :] * along_v[half]
        )
        lh[half * LINES : (half + 1) * LINES, :] = r0b[0:LINES, :] * across[half]

    def scatter(step, _):
        at = pl.multiple_of(step * NB, NB)
        value = dot_nt(lc[...], c0t[pl.ds(at, NB), :])
        slope = dot_nt(lh[...], c1t[pl.ds(at, NB), :])
        grad[0, :, pl.ds(at, NB)] = (value[0:LINES] + value[LINES : 2 * LINES]) + (
            slope[0:LINES] + slope[LINES:]
        )
        grad[1, :, pl.ds(at, NB)] = value[2 * LINES : 3 * LINES] + value[3 * LINES :]
        return _

    lax.fori_loop(0, NY // NB, scatter, 0)

    def project(group):
        finish(edges_back(group))
        for h in range(PER):
            c = group * PER + h
            pieces = []
            row = lax.broadcasted_iota(I32, (RX, NY), 0)
            for k in range(LB):
                lev = c * LB + k
                at = pl.multiple_of(lev * RX, RX)
                gradients = []
                for w in range(2):
                    edge = w * (EDGE // 2) + h * LB + k
                    first = jnp.where(has_prev, gtop[group, edge : edge + 1, :], 0.0)
                    last = jnp.where(has_next, gbot[group, edge : edge + 1, :], 0.0)
                    gradients.append(
                        grad[w, pl.ds(at, RX), :]
                        + jnp.where(row == 0, first, jnp.where(row == RX - 1, last, 0.0))
                    )
                for m in range(M):
                    pieces.append(
                        gradients[0] * pert[m, 0, lev].astype(F32)
                        + gradients[1] * pert[m, 1, lev].astype(F32)
                    )
            high, low = split(jnp.concatenate(pieces, axis=0))
            at = pl.multiple_of(c * (ROWS * RX), ROWS * RX)
            value = dot(jnp.concatenate([high, low], axis=0), pyt[...])
            part[pl.ds(at, ROWS * RX), :] = value[: ROWS * RX] + value[ROWS * RX :]
            f = [part[pl.ds(at + i, ROWS, stride=RX), :] for i in range(RX)]
            taps = (0.125, 0.375, 0.625, 0.875, 0.875, 0.625, 0.375, 0.125)
            rows = {}
            for q in range(-1, R + 1):
                value = None
                for t, tap in enumerate(taps):
                    i = 4 * q - 2 + t
                    if 0 <= i < RX:
                        term = (diffuse * diffuse * tap) * f[i]
                        value = term if value is None else value + term
                rows[q] = inside(q, value)
            rows = one_pass(rows, -2, R + 1, inside)
            rows = one_pass(rows, -3, R + 2, inside)
            at = pl.multiple_of(c * ROWS, ROWS)
            for k in range(3):
                sdn[k, pl.ds(at, ROWS), :] = rows[k - 3]
                sup[k, pl.ds(at, ROWS), :] = rows[R + k]
            for k in range(LB):
                for r in range(R):
                    out_ref[pl.ds((c * LB + k) * R + r, M, stride=L * R), :] = rows[r][
                        k * M : (k + 1) * M
                    ]
            begin(rims_out(c))

    each(GROUPS, project)

    def collect(c):
        finish(rims_out(c))
        for k in range(LB):
            at = pl.multiple_of(c * ROWS + k * M, M)
            for r in range(R):
                value = 0.0
                if r < 3:
                    value = value + jnp.where(has_prev, qup[r, pl.ds(at, M), :], 0.0)
                if r >= R - 3:
                    value = value + jnp.where(has_next, qdn[r - (R - 3), pl.ds(at, M), :], 0.0)
                rest_ref[pl.ds((c * LB + k) * R + r, M, stride=L * R), :] = value

    each(CHUNKS, collect)


def local(regions, members, alpha, perturbation, obs_cell, obs_kind, obs_value, obs_weight):
    any_space = pl.BlockSpec(memory_space=pl.ANY)
    in_vmem = pl.BlockSpec(memory_space=pltpu.VMEM)
    row = (1, OBS)
    edge = pltpu.VMEM((GROUPS, EDGE, NY), F32)
    rows3 = pltpu.VMEM((3, M * L, C), F32)

    def stream(rows):
        one = pltpu.VMEM((rows, OBS), F32)
        return (
            one,
            pltpu.VMEM((YS - 1, rows, OBS), F32),
            one,
            pltpu.VMEM((ZS - 1, rows, OBS), F32),
        )

    out, rest = pl.pallas_call(
        functools.partial(kernel, 1.0 / math.sqrt(members), regions),
        out_shape=[jax.ShapeDtypeStruct((M * L * R, C), F32)] * 2,
        in_specs=[any_space, any_space] + [in_vmem] * 4,
        out_specs=[in_vmem] * 2,
        scratch_shapes=[
            pltpu.VMEM((M, 2, L, RX, NY), BF16),
            pltpu.VMEM((M, L * R, C), F32),
            pltpu.VMEM((R + 6, M * L, C), F32),
            pltpu.VMEM((M * L * RX, C), F32),
            pltpu.VMEM((NY, OBS), BF16),
            pltpu.VMEM((NY, OBS), BF16),
            pltpu.VMEM((LINES, OBS), F32),
            pltpu.VMEM((LINES, OBS), F32),
            pltpu.VMEM((LINES, OBS), BF16),
            pltpu.VMEM((LINES, OBS), BF16),
            pltpu.VMEM((2 * GROUPS * EDGE, OBS), F32),
            pltpu.VMEM((2 * GROUPS * EDGE, OBS), BF16),
            pltpu.VMEM((2 * C, NY), BF16),
            pltpu.VMEM((NY, C), BF16),
            pltpu.VMEM((4, LINES, NY), BF16),
            edge,
            edge,
            edge,
            edge,
            tuple(stream(rows) for rows in (3, 1)),
            pltpu.VMEM((4 * LINES, OBS), BF16),
            pltpu.VMEM((2 * LINES, OBS), BF16),
            edge,
            edge,
            edge,
            edge,
            pltpu.VMEM((2, LINES, NY), F32),
            rows3,
            rows3,
            rows3,
            rows3,
            pltpu.SemaphoreType.DMA((1 + CHUNKS,)),
            pltpu.SemaphoreType.DMA((4 * CHUNKS + 4 * GROUPS + 12,)),
            pltpu.SemaphoreType.DMA((4 * CHUNKS + 4 * GROUPS + 12,)),
        ],
        compiler_params=pltpu.CompilerParams(
            collective_id=0, has_side_effects=True, vmem_limit_bytes=62 * 1024 * 1024
        ),
    )(
        alpha.reshape(M, L * R, C),
        perturbation,
        obs_cell.reshape(row),
        obs_kind.reshape(row),
        obs_value.reshape(row),
        obs_weight.reshape(row),
    )
    return (out + rest).reshape(M, L, R, C)


def solution(mesh):
    regions, groups = mesh.shape["reg"], mesh.shape["mem"]
    return jax.shard_map(
        functools.partial(local, regions, M * groups),
        mesh=mesh,
        in_specs=(
            P("mem", None, "reg", None),
            P("mem", None, None, "reg", None),
            P("reg"),
            P("reg"),
            P("reg"),
            P("reg"),
        ),
        out_specs=P("mem", None, "reg", None),
        check_vma=False,
    )
```

```python
import functools
import math

import jax
import jax.numpy as jnp
from jax import lax
from jax.experimental import pallas as pl
from jax.experimental.pallas import tpu as pltpu
from jax.sharding import PartitionSpec as P

MESH = pl.DeviceIdType.MESH
F32, BF16, I32 = jnp.float32, jnp.bfloat16, jnp.int32
diffuse = 0.2

YS = 4
ZS = 4
M, L, R, C = 8, 16, 4, 128
RX, NY, OBS = 16, 512, 1024
LINES = L * RX
LB = 2
CHUNKS = L // LB
ROWS = LB * M
GROUPS = 4
PER = CHUNKS // GROUPS
EDGE = 2 * (L // GROUPS)
NT = (((1,), (1,)), ((), ()))


def split(value):
    high = value.astype(BF16)
    return high, (value - high.astype(F32)).astype(BF16)


def dot(a, b):
    return jnp.dot(a, b, preferred_element_type=F32)


def dot_nt(a, b):
    return lax.dot_general(a, b, NT, preferred_element_type=F32)


def sides(value):
    lane = lax.broadcasted_iota(I32, value.shape, 1)
    left = jnp.where(lane == 0, 0.0, pltpu.roll(value, 1, 1))
    right = jnp.where(lane == C - 1, 0.0, pltpu.roll(value, C - 1, 1))
    return left + right


def one_pass(rows, first, last, inside):
    out = {}
    for k in range(first, last + 1):
        value = None
        for near in (k - 1, k, k + 1):
            if near in rows:
                value = rows[near] if value is None else value + rows[near]
        if k in rows:
            value = value + sides(rows[k])
        out[k] = inside(k, value)
    return out


def kernel(
    scale,
    regions,
    alpha_hbm,
    pert_hbm,
    cell_ref,
    kind_ref,
    val_ref,
    wt_ref,
    out_ref,
    rest_ref,
    pert,
    alpha,
    slab,
    part,
    c0t,
    c1t,
    r0f,
    r1f,
    r0b,
    r1b,
    rimf,
    rimb,
    py2,
    pyt,
    fields,
    etop,
    ebot,
    rtop,
    rbot,
    streams,
    lc,
    lh,
    ftop,
    fbot,
    gtop,
    gbot,
    grad,
    sup,
    sdn,
    qup,
    qdn,
    local_sem,
    send_sem,
    recv_sem,
    far_sem,
):
    mem = lax.axis_index("mem")
    reg = lax.axis_index("reg")
    y, zh = lax.rem(mem, YS), mem // YS
    up = lax.rem(reg + 1, regions)
    down = lax.rem(reg + regions - 1, regions)
    has_prev = reg > 0
    has_next = reg < regions - 1
    y_peers = [zh * YS + lax.rem(y + d, YS) for d in range(1, YS)]
    z_peers = [lax.rem(zh + d, ZS) * YS + y for d in range(1, ZS)]

    def remote(source, target, index, **where):
        return pltpu.make_async_remote_copy(
            src_ref=source,
            dst_ref=target,
            send_sem=send_sem.at[index],
            recv_sem=recv_sem.at[index],
            device_id=where,
            device_id_type=MESH,
        )

    def send(*args, **where):
        copy = remote(*args, **where)
        copy.start()
        return copy

    def rims_in(c):
        at = pl.ds(pl.multiple_of(c * ROWS, ROWS), ROWS)
        return (
            remote(slab.at[pl.ds(4, 3), at], slab.at[pl.ds(0, 3), at], c, reg=up),
            remote(slab.at[pl.ds(3, 3), at], slab.at[pl.ds(7, 3), at], CHUNKS + c, reg=down),
        )

    def rims_out(c):
        at = pl.ds(pl.multiple_of(c * ROWS, ROWS), ROWS)
        first = 2 * CHUNKS
        return (
            remote(sdn.at[:, at], qdn.at[:, at], first + c, reg=down),
            remote(sup.at[:, at], qup.at[:, at], first + CHUNKS + c, reg=up),
        )

    def edges(g):
        first = 4 * CHUNKS
        return (
            remote(etop.at[g], rbot.at[g], first + g, reg=down),
            remote(ebot.at[g], rtop.at[g], first + GROUPS + g, reg=up),
        )

    def edges_back(g):
        first = 4 * CHUNKS + 2 * GROUPS
        return (
            remote(ftop.at[g], gbot.at[g], first + g, reg=down),
            remote(fbot.at[g], gtop.at[g], first + GROUPS + g, reg=up),
        )

    fields_out, along_out = streams[0][0], streams[1][0]
    sums = 4 * CHUNKS + 4 * GROUPS

    def y_copies(n):
        mine, from_y = streams[n][0], streams[n][1]
        return [
            remote(mine, from_y.at[d], sums + 6 * n + d, mem=who) for d, who in enumerate(y_peers)
        ]

    def z_copies(n):
        held, from_z = streams[n][2], streams[n][3]
        return [
            remote(held, from_z.at[d], sums + 6 * n + 3 + d, mem=who)
            for d, who in reversed(list(enumerate(z_peers)))
        ]

    def y_start(n):
        begin(y_copies(n))

    def y_end(n):
        mine, from_y, held = streams[n][:3]
        finish(y_copies(n))
        total = mine[...]
        for d in range(YS - 1):
            total = total + from_y[d]
        held[...] = total
        begin(z_copies(n))

    def z_end(n):
        held, from_z = streams[n][2:]
        finish(z_copies(n))
        total = held[...]
        for d in range(ZS - 1):
            total = total + from_z[d]
        return total

    def begin(copies):
        for copy in copies:
            copy.start()

    def finish(copies):
        for copy in copies:
            copy.wait()

    def each(count, body):
        def step(i, _):
            body(i)
            return _

        lax.fori_loop(0, count, step, 0)

    barrier = pltpu.get_barrier_semaphore()
    for who in (up, down):
        pl.semaphore_signal(barrier, inc=1, device_id={"reg": who}, device_id_type=MESH)
    z_up, z_down = z_peers[0], z_peers[-1]
    for who in y_peers + [z_up, z_down]:
        pl.semaphore_signal(barrier, inc=1, device_id={"mem": who}, device_id_type=MESH)
    def get_alpha(c):
        at = pl.ds(pl.multiple_of(c * (LB * R), LB * R), LB * R)
        return pltpu.make_async_copy(alpha_hbm.at[:, at], alpha.at[:, at], local_sem.at[1 + c])

    each(CHUNKS, lambda c: get_alpha(c).start())
    get_pert = pltpu.make_async_copy(pert_hbm, pert, local_sem.at[0])
    get_pert.start()
    pl.semaphore_wait(barrier, 2 + YS - 1 + 2)
    pl.semaphore_signal(far_sem, inc=1, device_id={"mem": z_down}, device_id_type=MESH)
    flat = alpha.reshape(M * L * R, C)

    def arrange(c):
        get_alpha(c).wait()
        for k in range(LB):
            lev = c * LB + k
            at = pl.multiple_of(lev * M, M)
            for r in range(R):
                slab[3 + r, pl.ds(at, M), :] = flat[pl.ds(lev * R + r, M, stride=L * R), :]
        begin(rims_in(c))

    each(CHUNKS, arrange)

    cell = cell_ref[...]
    kind = kind_ref[...]
    column = cell & (NY - 1)
    row_in = (cell >> 9) & (RX - 1)
    level = cell >> 13
    line = cell >> 9
    line_m = jnp.where(row_in > 0, line - 1, -1)
    line_p = jnp.where(row_in < RX - 1, line + 1, -1)
    per = L // GROUPS
    place = (level // per) * EDGE + level % per + jnp.where(kind == 2, per, 0)
    place = jnp.where(row_in == 0, place, GROUPS * EDGE + place)
    place = jnp.where((kind >= 2) & ((row_in == 0) | (row_in == RX - 1)), place, -1)
    number = lax.broadcasted_iota(I32, (2 * GROUPS * EDGE, OBS), 0)
    outer = jnp.where(number == place, jnp.where(row_in == 0, -0.5, 0.5), 0.0)
    rimf[...] = outer
    rimb[...] = outer.astype(BF16)

    def build_columns(step, _):
        at = pl.multiple_of(step * 32, 32)
        number = lax.broadcasted_iota(I32, (32, OBS), 0) + at
        c0t[pl.ds(at, 32), :] = jnp.where(number == column, 1.0, 0.0).astype(BF16)
        c1t[pl.ds(at, 32), :] = jnp.where(
            number == column + 1, 0.5, jnp.where(number == column - 1, -0.5, 0.0)
        ).astype(BF16)
        return _

    lax.fori_loop(0, NY // 32, build_columns, 0)

    def build_lines(step, _):
        at = pl.multiple_of(step * 32, 32)
        number = lax.broadcasted_iota(I32, (32, OBS), 0) + at
        r0 = jnp.where(number == line, 1.0, 0.0)
        r1 = jnp.where(number == line_p, 0.5, jnp.where(number == line_m, -0.5, 0.0))
        r0f[pl.ds(at, 32), :] = r0
        r1f[pl.ds(at, 32), :] = r1
        r0b[pl.ds(at, 32), :] = r0.astype(BF16)
        r1b[pl.ds(at, 32), :] = r1.astype(BF16)
        return _

    lax.fori_loop(0, LINES // 32, build_lines, 0)

    def table(shape, fine_dim):
        fine = lax.broadcasted_iota(I32, shape, fine_dim).astype(F32)
        coarse = lax.broadcasted_iota(I32, shape, 1 - fine_dim).astype(F32)
        return jnp.maximum(0.0, 1.0 - jnp.abs((fine + 0.5) / 4.0 - 0.5 - coarse)).astype(BF16)

    weights = table((C, NY), 1)
    py2[0:C, :] = weights
    py2[C : 2 * C, :] = weights
    pyt[...] = table((NY, C), 0)

    def inside(k, value):
        if k < 0:
            return jnp.where(has_prev, value, 0.0)
        if k >= R:
            return jnp.where(has_next, value, 0.0)
        return value

    get_pert.wait()

    def increments(group):
        for h in range(PER):
            c = group * PER + h
            finish(rims_in(c))
            at = pl.multiple_of(c * ROWS, ROWS)
            rows = {k - 3: inside(k - 3, slab[k, pl.ds(at, ROWS), :]) for k in range(R + 6)}
            rows = one_pass(rows, -2, R + 1, inside)
            rows = one_pass(rows, -1, R, inside)
            at = pl.multiple_of(c * (ROWS * RX), ROWS * RX)
            for i in range(RX):
                q, s = divmod(i, 4)
                mine, other = ((0.625, 0.375), (0.875, 0.125), (0.875, 0.125), (0.625, 0.375))[s]
                near = q - 1 if s < 2 else q + 1
                part[pl.ds(at + i, ROWS, stride=RX), :] = (diffuse * diffuse * mine) * rows[q] + (
                    diffuse * diffuse * other
                ) * rows[near]
            high, low = split(part[pl.ds(at, ROWS * RX), :])
            fine = dot(jnp.concatenate([high, low], axis=1), py2[...])
            for k in range(LB):
                lev = c * LB + k
                for w in range(2):
                    total = None
                    for m in range(M):
                        at = (k * M + m) * RX
                        term = fine[at : at + RX] * pert[m, w, lev].astype(F32)
                        total = term if total is None else total + term
                    at = pl.multiple_of(lev * RX, RX)
                    fields[2 * w, pl.ds(at, RX), :], fields[2 * w + 1, pl.ds(at, RX), :] = split(total)
                    row = w * (EDGE // 2) + h * LB + k
                    etop[group, row : row + 1, :] = total[0:1]
                    ebot[group, row : row + 1, :] = total[RX - 1 : RX]
        begin(edges(group))

    each(GROUPS, increments)

    NB = 256

    def pick(step, _):
        at = pl.multiple_of(step * NB, NB)
        at = pl.ds(at, NB)
        second = kind_ref[:, at] == 2
        on, beside = r0f[:, at], r1f[:, at]

        def over(lines):
            return jnp.sum(lines, axis=0, keepdims=True)

        value = dot(fields[...].reshape(4 * LINES, NY), c0t[:, at])
        at_u = value[0:LINES] + value[LINES : 2 * LINES]
        at_v = value[2 * LINES : 3 * LINES] + value[3 * LINES :]
        fields_out[0:1, at] = over(on * at_u)
        fields_out[1:2, at] = over(on * at_v)
        along_out[:, at] = over(beside * jnp.where(second, at_v, at_u))
        value = dot(fields[0:2].reshape(2 * LINES, NY), c1t[:, at])
        fields_out[2:3, at] = over(on * (value[0:LINES] + value[LINES:]))
        return _

    lax.fori_loop(0, OBS // NB, pick, 0)
    y_start(0)
    each(GROUPS, lambda g: finish(edges(g)))
    sides_in = [
        jnp.where(has_prev, rtop[...].reshape(GROUPS * EDGE, NY), 0.0),
        jnp.where(has_next, rbot[...].reshape(GROUPS * EDGE, NY), 0.0),
    ]
    high, low = split(jnp.concatenate(sides_in, axis=0))
    rim = dot(high, c0t[...]) + dot(low, c0t[...])
    along_out[...] = along_out[...] + jnp.sum(rimf[...] * rim, axis=0, keepdims=True)
    y_start(1)

    pl.semaphore_wait(far_sem, 1)
    y_end(0)
    y_end(1)
    total, slope_x = z_end(0) * scale, z_end(1) * scale
    u, v, slope_y = total[0:1], total[1:2], total[2:3]
    is_u, is_v, is_vort, is_adv = kind == 0, kind == 1, kind == 2, kind == 3
    seen = jnp.where(
        is_u,
        u,
        jnp.where(is_v, v, jnp.where(is_vort, slope_x - slope_y, u * slope_x + v * slope_y)),
    )
    misfit = wt_ref[...] * (seen - val_ref[...]) * scale
    zero = jnp.zeros_like(misfit)
    to_u = split(jnp.where(is_u, misfit, jnp.where(is_adv, misfit * slope_x, zero)))
    to_v = split(jnp.where(is_v, misfit, jnp.where(is_adv, misfit * slope_y, zero)))
    along_u = split(jnp.where(is_adv, misfit * u, zero))
    along_v = split(jnp.where(is_vort, misfit, zero))
    across = split(jnp.where(is_vort, -misfit, jnp.where(is_adv, misfit * v, zero)))

    high = rimb[...] * (along_u[0] + along_v[0])
    low = rimb[...] * (along_u[1] + along_v[1])
    rim = dot_nt(high, c0t[...]) + dot_nt(low, c0t[...])
    ftop[...] = rim[: GROUPS * EDGE].reshape(GROUPS, EDGE, NY)
    fbot[...] = rim[GROUPS * EDGE :].reshape(GROUPS, EDGE, NY)
    each(GROUPS, lambda g: begin(edges_back(g)))

    for half in range(2):
        lc[half * LINES : (half + 1) * LINES, :] = (
            r0b[0:LINES, :] * to_u[half] + r1b[0:LINES, :] * along_u[half]
        )
        lc[(2 + half) * LINES : (3 + half) * LINES, :] = (
            r0b[0:LINES, :] * to_v[half] + r1b[0:LINES, :] * along_v[half]
        )
        lh[half * LINES : (half + 1) * LINES, :] = r0b[0:LINES, :] * across[half]

    def scatter(step, _):
        at = pl.multiple_of(step * NB, NB)
        value = dot_nt(lc[...], c0t[pl.ds(at, NB), :])
        slope = dot_nt(lh[...], c1t[pl.ds(at, NB), :])
        grad[0, :, pl.ds(at, NB)] = (value[0:LINES] + value[LINES : 2 * LINES]) + (
            slope[0:LINES] + slope[LINES:]
        )
        grad[1, :, pl.ds(at, NB)] = value[2 * LINES : 3 * LINES] + value[3 * LINES :]
        return _

    lax.fori_loop(0, NY // NB, scatter, 0)

    def project(group):
        finish(edges_back(group))
        for h in range(PER):
            c = group * PER + h
            pieces = []
            row = lax.broadcasted_iota(I32, (RX, NY), 0)
            for k in range(LB):
                lev = c * LB + k
                at = pl.multiple_of(lev * RX, RX)
                gradients = []
                for w in range(2):
                    edge = w * (EDGE // 2) + h * LB + k
                    first = jnp.where(has_prev, gtop[group, edge : edge + 1, :], 0.0)
                    last = jnp.where(has_next, gbot[group, edge : edge + 1, :], 0.0)
                    gradients.append(
                        grad[w, pl.ds(at, RX), :]
                        + jnp.where(row == 0, first, jnp.where(row == RX - 1, last, 0.0))
                    )
                for m in range(M):
                    pieces.append(
                        gradients[0] * pert[m, 0, lev].astype(F32)
                        + gradients[1] * pert[m, 1, lev].astype(F32)
                    )
            high, low = split(jnp.concatenate(pieces, axis=0))
            at = pl.multiple_of(c * (ROWS * RX), ROWS * RX)
            value = dot(jnp.concatenate([high, low], axis=0), pyt[...])
            part[pl.ds(at, ROWS * RX), :] = value[: ROWS * RX] + value[ROWS * RX :]
            f = [part[pl.ds(at + i, ROWS, stride=RX), :] for i in range(RX)]
            taps = (0.125, 0.375, 0.625, 0.875, 0.875, 0.625, 0.375, 0.125)
            rows = {}
            for q in range(-1, R + 1):
                value = None
                for t, tap in enumerate(taps):
                    i = 4 * q - 2 + t
                    if 0 <= i < RX:
                        term = (diffuse * diffuse * tap) * f[i]
                        value = term if value is None else value + term
                rows[q] = inside(q, value)
            rows = one_pass(rows, -2, R + 1, inside)
            rows = one_pass(rows, -3, R + 2, inside)
            at = pl.multiple_of(c * ROWS, ROWS)
            for k in range(3):
                sdn[k, pl.ds(at, ROWS), :] = rows[k - 3]
                sup[k, pl.ds(at, ROWS), :] = rows[R + k]
            for k in range(LB):
                for r in range(R):
                    out_ref[pl.ds((c * LB + k) * R + r, M, stride=L * R), :] = rows[r][
                        k * M : (k + 1) * M
                    ]
            begin(rims_out(c))

    each(GROUPS, project)

    def collect(c):
        finish(rims_out(c))
        for k in range(LB):
            at = pl.multiple_of(c * ROWS + k * M, M)
            for r in range(R):
                value = 0.0
                if r < 3:
                    value = value + jnp.where(has_prev, qup[r, pl.ds(at, M), :], 0.0)
                if r >= R - 3:
                    value = value + jnp.where(has_next, qdn[r - (R - 3), pl.ds(at, M), :], 0.0)
                rest_ref[pl.ds((c * LB + k) * R + r, M, stride=L * R), :] = value

    each(CHUNKS, collect)


def local(regions, members, alpha, perturbation, obs_cell, obs_kind, obs_value, obs_weight):
    any_space = pl.BlockSpec(memory_space=pl.ANY)
    in_vmem = pl.BlockSpec(memory_space=pltpu.VMEM)
    row = (1, OBS)
    edge = pltpu.VMEM((GROUPS, EDGE, NY), F32)
    rows3 = pltpu.VMEM((3, M * L, C), F32)

    def stream(rows):
        one = pltpu.VMEM((rows, OBS), F32)
        return (
            one,
            pltpu.VMEM((YS - 1, rows, OBS), F32),
            one,
            pltpu.VMEM((ZS - 1, rows, OBS), F32),
        )

    out, rest = pl.pallas_call(
        functools.partial(kernel, 1.0 / math.sqrt(members), regions),
        out_shape=[jax.ShapeDtypeStruct((M * L * R, C), F32)] * 2,
        in_specs=[any_space, any_space] + [in_vmem] * 4,
        out_specs=[in_vmem] * 2,
        scratch_shapes=[
            pltpu.VMEM((M, 2, L, RX, NY), BF16),
            pltpu.VMEM((M, L * R, C), F32),
            pltpu.VMEM((R + 6, M * L, C), F32),
            pltpu.VMEM((M * L * RX, C), F32),
            pltpu.VMEM((NY, OBS), BF16),
            pltpu.VMEM((NY, OBS), BF16),
            pltpu.VMEM((LINES, OBS), F32),
            pltpu.VMEM((LINES, OBS), F32),
            pltpu.VMEM((LINES, OBS), BF16),
            pltpu.VMEM((LINES, OBS), BF16),
            pltpu.VMEM((2 * GROUPS * EDGE, OBS), F32),
            pltpu.VMEM((2 * GROUPS * EDGE, OBS), BF16),
            pltpu.VMEM((2 * C, NY), BF16),
            pltpu.VMEM((NY, C), BF16),
            pltpu.VMEM((4, LINES, NY), BF16),
            edge,
            edge,
            edge,
            edge,
            tuple(stream(rows) for rows in (3, 1)),
            pltpu.VMEM((4 * LINES, OBS), BF16),
            pltpu.VMEM((2 * LINES, OBS), BF16),
            edge,
            edge,
            edge,
            edge,
            pltpu.VMEM((2, LINES, NY), F32),
            rows3,
            rows3,
            rows3,
            rows3,
            pltpu.SemaphoreType.DMA((1 + CHUNKS,)),
            pltpu.SemaphoreType.DMA((4 * CHUNKS + 4 * GROUPS + 12,)),
            pltpu.SemaphoreType.DMA((4 * CHUNKS + 4 * GROUPS + 12,)),
            pltpu.SemaphoreType.REGULAR,
        ],
        compiler_params=pltpu.CompilerParams(
            collective_id=0, has_side_effects=True, vmem_limit_bytes=62 * 1024 * 1024
        ),
    )(
        alpha.reshape(M, L * R, C),
        perturbation,
        obs_cell.reshape(row),
        obs_kind.reshape(row),
        obs_value.reshape(row),
        obs_weight.reshape(row),
    )
    return (out + rest).reshape(M, L, R, C)


def solution(mesh):
    regions, groups = mesh.shape["reg"], mesh.shape["mem"]
    return jax.shard_map(
        functools.partial(local, regions, M * groups),
        mesh=mesh,
        in_specs=(
            P("mem", None, "reg", None),
            P("mem", None, None, "reg", None),
            P("reg"),
            P("reg"),
            P("reg"),
            P("reg"),
        ),
        out_specs=P("mem", None, "reg", None),
        check_vma=False,
    )
```

```python
import functools
import math

import jax
import jax.numpy as jnp
from jax import lax
from jax.experimental import pallas as pl
from jax.experimental.pallas import tpu as pltpu
from jax.sharding import PartitionSpec as P

MESH = pl.DeviceIdType.MESH
F32, BF16, I32 = jnp.float32, jnp.bfloat16, jnp.int32
diffuse = 0.2

YS = 4
ZS = 4
M, L, R, C = 8, 16, 4, 128
RX, NY, OBS = 16, 512, 1024
LINES = L * RX
LB = 2
CHUNKS = L // LB
ROWS = LB * M
GROUPS = 4
PER = CHUNKS // GROUPS
EDGE = 2 * (L // GROUPS)
NT = (((1,), (1,)), ((), ()))


def split(value):
    high = value.astype(BF16)
    return high, (value - high.astype(F32)).astype(BF16)


def dot(a, b):
    return jnp.dot(a, b, preferred_element_type=F32)


def dot_nt(a, b):
    return lax.dot_general(a, b, NT, preferred_element_type=F32)


def sides(value):
    lane = lax.broadcasted_iota(I32, value.shape, 1)
    left = jnp.where(lane == 0, 0.0, pltpu.roll(value, 1, 1))
    right = jnp.where(lane == C - 1, 0.0, pltpu.roll(value, C - 1, 1))
    return left + right


def one_pass(rows, first, last, inside):
    out = {}
    for k in range(first, last + 1):
        value = None
        for near in (k - 1, k, k + 1):
            if near in rows:
                value = rows[near] if value is None else value + rows[near]
        if k in rows:
            value = value + sides(rows[k])
        out[k] = inside(k, value)
    return out


def kernel(
    scale,
    regions,
    alpha_hbm,
    pert_hbm,
    cell_hbm,
    kind_hbm,
    val_hbm,
    wt_hbm,
    out_hbm,
    rest_hbm,
    cell_ref,
    kind_ref,
    val_ref,
    wt_ref,
    out_ref,
    rest_ref,
    pert,
    alpha,
    slab,
    part,
    c0t,
    c1t,
    r0f,
    r1f,
    r0b,
    r1b,
    rimf,
    rimb,
    py2,
    pyt,
    fields,
    etop,
    ebot,
    rtop,
    rbot,
    streams,
    lc,
    lh,
    ftop,
    fbot,
    gtop,
    gbot,
    grad,
    sup,
    sdn,
    qup,
    qdn,
    local_sem,
    send_sem,
    recv_sem,
    far_sem,
):
    mem = lax.axis_index("mem")
    reg = lax.axis_index("reg")
    y, zh = lax.rem(mem, YS), mem // YS
    up = lax.rem(reg + 1, regions)
    down = lax.rem(reg + regions - 1, regions)
    has_prev = reg > 0
    has_next = reg < regions - 1
    y_peers = [zh * YS + lax.rem(y + d, YS) for d in range(1, YS)]
    z_peers = [lax.rem(zh + d, ZS) * YS + y for d in range(1, ZS)]

    def remote(source, target, index, **where):
        return pltpu.make_async_remote_copy(
            src_ref=source,
            dst_ref=target,
            send_sem=send_sem.at[index],
            recv_sem=recv_sem.at[index],
            device_id=where,
            device_id_type=MESH,
        )

    def send(*args, **where):
        copy = remote(*args, **where)
        copy.start()
        return copy

    def rims_in(c):
        at = pl.ds(pl.multiple_of(c * ROWS, ROWS), ROWS)
        return (
            remote(slab.at[pl.ds(4, 3), at], slab.at[pl.ds(0, 3), at], c, reg=up),
            remote(slab.at[pl.ds(3, 3), at], slab.at[pl.ds(7, 3), at], CHUNKS + c, reg=down),
        )

    def rims_out(c):
        at = pl.ds(pl.multiple_of(c * ROWS, ROWS), ROWS)
        first = 2 * CHUNKS
        return (
            remote(sdn.at[:, at], qdn.at[:, at], first + c, reg=down),
            remote(sup.at[:, at], qup.at[:, at], first + CHUNKS + c, reg=up),
        )

    def edges(g):
        first = 4 * CHUNKS
        return (
            remote(etop.at[g], rbot.at[g], first + g, reg=down),
            remote(ebot.at[g], rtop.at[g], first + GROUPS + g, reg=up),
        )

    def edges_back(g):
        first = 4 * CHUNKS + 2 * GROUPS
        return (
            remote(ftop.at[g], gbot.at[g], first + g, reg=down),
            remote(fbot.at[g], gtop.at[g], first + GROUPS + g, reg=up),
        )

    fields_out, along_out = streams[0][0], streams[1][0]
    sums = 4 * CHUNKS + 4 * GROUPS

    def y_copies(n):
        mine, from_y = streams[n][0], streams[n][1]
        return [
            remote(mine, from_y.at[d], sums + 6 * n + d, mem=who) for d, who in enumerate(y_peers)
        ]

    def z_copies(n):
        held, from_z = streams[n][2], streams[n][3]
        return [
            remote(held, from_z.at[d], sums + 6 * n + 3 + d, mem=who)
            for d, who in reversed(list(enumerate(z_peers)))
        ]

    def y_start(n):
        begin(y_copies(n))

    def y_end(n):
        mine, from_y, held = streams[n][:3]
        finish(y_copies(n))
        total = mine[...]
        for d in range(YS - 1):
            total = total + from_y[d]
        held[...] = total
        begin(z_copies(n))

    def z_end(n):
        held, from_z = streams[n][2:]
        finish(z_copies(n))
        total = held[...]
        for d in range(ZS - 1):
            total = total + from_z[d]
        return total

    def begin(copies):
        for copy in copies:
            copy.start()

    def finish(copies):
        for copy in copies:
            copy.wait()

    def each(count, body):
        def step(i, _):
            body(i)
            return _

        lax.fori_loop(0, count, step, 0)

    barrier = pltpu.get_barrier_semaphore()
    for who in (up, down):
        pl.semaphore_signal(barrier, inc=1, device_id={"reg": who}, device_id_type=MESH)
    z_up, z_down = z_peers[0], z_peers[-1]
    for who in y_peers + [z_up, z_down]:
        pl.semaphore_signal(barrier, inc=1, device_id={"mem": who}, device_id_type=MESH)
    def get_alpha(c):
        at = pl.ds(pl.multiple_of(c * (LB * R), LB * R), LB * R)
        return pltpu.make_async_copy(alpha_hbm.at[:, at], alpha.at[:, at], local_sem.at[1 + c])

    each(CHUNKS, lambda c: get_alpha(c).start())
    get_pert = pltpu.make_async_copy(pert_hbm, pert, local_sem.at[0])
    get_pert.start()
    get_obs = [
        pltpu.make_async_copy(source, target, local_sem.at[1 + CHUNKS + n])
        for n, (source, target) in enumerate(
            ((cell_hbm, cell_ref), (kind_hbm, kind_ref), (val_hbm, val_ref), (wt_hbm, wt_ref))
        )
    ]
    begin(get_obs)
    pl.semaphore_wait(barrier, 2 + YS - 1 + 2)
    pl.semaphore_signal(far_sem, inc=1, device_id={"mem": z_down}, device_id_type=MESH)
    flat = alpha.reshape(M * L * R, C)

    def arrange(c):
        get_alpha(c).wait()
        for k in range(LB):
            lev = c * LB + k
            at = pl.multiple_of(lev * M, M)
            for r in range(R):
                slab[3 + r, pl.ds(at, M), :] = flat[pl.ds(lev * R + r, M, stride=L * R), :]
        begin(rims_in(c))

    each(CHUNKS, arrange)

    finish(get_obs)
    cell = cell_ref[...]
    kind = kind_ref[...]
    column = cell & (NY - 1)
    row_in = (cell >> 9) & (RX - 1)
    level = cell >> 13
    line = cell >> 9
    line_m = jnp.where(row_in > 0, line - 1, -1)
    line_p = jnp.where(row_in < RX - 1, line + 1, -1)
    per = L // GROUPS
    place = (level // per) * EDGE + level % per + jnp.where(kind == 2, per, 0)
    place = jnp.where(row_in == 0, place, GROUPS * EDGE + place)
    place = jnp.where((kind >= 2) & ((row_in == 0) | (row_in == RX - 1)), place, -1)
    number = lax.broadcasted_iota(I32, (2 * GROUPS * EDGE, OBS), 0)
    outer = jnp.where(number == place, jnp.where(row_in == 0, -0.5, 0.5), 0.0)
    rimf[...] = outer
    rimb[...] = outer.astype(BF16)

    def build_columns(step, _):
        at = pl.multiple_of(step * 32, 32)
        number = lax.broadcasted_iota(I32, (32, OBS), 0) + at
        c0t[pl.ds(at, 32), :] = jnp.where(number == column, 1.0, 0.0).astype(BF16)
        c1t[pl.ds(at, 32), :] = jnp.where(
            number == column + 1, 0.5, jnp.where(number == column - 1, -0.5, 0.0)
        ).astype(BF16)
        return _

    lax.fori_loop(0, NY // 32, build_columns, 0)

    def build_lines(step, _):
        at = pl.multiple_of(step * 32, 32)
        number = lax.broadcasted_iota(I32, (32, OBS), 0) + at
        r0 = jnp.where(number == line, 1.0, 0.0)
        r1 = jnp.where(number == line_p, 0.5, jnp.where(number == line_m, -0.5, 0.0))
        r0f[pl.ds(at, 32), :] = r0
        r1f[pl.ds(at, 32), :] = r1
        r0b[pl.ds(at, 32), :] = r0.astype(BF16)
        r1b[pl.ds(at, 32), :] = r1.astype(BF16)
        return _

    lax.fori_loop(0, LINES // 32, build_lines, 0)

    def table(shape, fine_dim):
        fine = lax.broadcasted_iota(I32, shape, fine_dim).astype(F32)
        coarse = lax.broadcasted_iota(I32, shape, 1 - fine_dim).astype(F32)
        return jnp.maximum(0.0, 1.0 - jnp.abs((fine + 0.5) / 4.0 - 0.5 - coarse)).astype(BF16)

    weights = table((C, NY), 1)
    py2[0:C, :] = weights
    py2[C : 2 * C, :] = weights
    pyt[...] = table((NY, C), 0)

    def inside(k, value):
        if k < 0:
            return jnp.where(has_prev, value, 0.0)
        if k >= R:
            return jnp.where(has_next, value, 0.0)
        return value

    get_pert.wait()

    def increments(group):
        for h in range(PER):
            c = group * PER + h
            finish(rims_in(c))
            at = pl.multiple_of(c * ROWS, ROWS)
            rows = {k - 3: inside(k - 3, slab[k, pl.ds(at, ROWS), :]) for k in range(R + 6)}
            rows = one_pass(rows, -2, R + 1, inside)
            rows = one_pass(rows, -1, R, inside)
            at = pl.multiple_of(c * (ROWS * RX), ROWS * RX)
            for i in range(RX):
                q, s = divmod(i, 4)
                mine, other = ((0.625, 0.375), (0.875, 0.125), (0.875, 0.125), (0.625, 0.375))[s]
                near = q - 1 if s < 2 else q + 1
                part[pl.ds(at + i, ROWS, stride=RX), :] = (diffuse * diffuse * mine) * rows[q] + (
                    diffuse * diffuse * other
                ) * rows[near]
            high, low = split(part[pl.ds(at, ROWS * RX), :])
            fine = dot(jnp.concatenate([high, low], axis=1), py2[...])
            for k in range(LB):
                lev = c * LB + k
                for w in range(2):
                    total = None
                    for m in range(M):
                        at = (k * M + m) * RX
                        term = fine[at : at + RX] * pert[m, w, lev].astype(F32)
                        total = term if total is None else total + term
                    at = pl.multiple_of(lev * RX, RX)
                    fields[2 * w, pl.ds(at, RX), :], fields[2 * w + 1, pl.ds(at, RX), :] = split(total)
                    row = w * (EDGE // 2) + h * LB + k
                    etop[group, row : row + 1, :] = total[0:1]
                    ebot[group, row : row + 1, :] = total[RX - 1 : RX]
        begin(edges(group))

    each(GROUPS, increments)

    NB = 256

    def pick(step, _):
        at = pl.multiple_of(step * NB, NB)
        at = pl.ds(at, NB)
        second = kind_ref[:, at] == 2
        on, beside = r0f[:, at], r1f[:, at]

        def over(lines):
            return jnp.sum(lines, axis=0, keepdims=True)

        value = dot(fields[...].reshape(4 * LINES, NY), c0t[:, at])
        at_u = value[0:LINES] + value[LINES : 2 * LINES]
        at_v = value[2 * LINES : 3 * LINES] + value[3 * LINES :]
        fields_out[0:1, at] = over(on * at_u)
        fields_out[1:2, at] = over(on * at_v)
        along_out[:, at] = over(beside * jnp.where(second, at_v, at_u))
        value = dot(fields[0:2].reshape(2 * LINES, NY), c1t[:, at])
        fields_out[2:3, at] = over(on * (value[0:LINES] + value[LINES:]))
        return _

    lax.fori_loop(0, OBS // NB, pick, 0)
    y_start(0)
    each(GROUPS, lambda g: finish(edges(g)))
    sides_in = [
        jnp.where(has_prev, rtop[...].reshape(GROUPS * EDGE, NY), 0.0),
        jnp.where(has_next, rbot[...].reshape(GROUPS * EDGE, NY), 0.0),
    ]
    high, low = split(jnp.concatenate(sides_in, axis=0))
    rim = dot(high, c0t[...]) + dot(low, c0t[...])
    along_out[...] = along_out[...] + jnp.sum(rimf[...] * rim, axis=0, keepdims=True)
    y_start(1)

    pl.semaphore_wait(far_sem, 1)
    y_end(0)
    y_end(1)
    total, slope_x = z_end(0) * scale, z_end(1) * scale
    u, v, slope_y = total[0:1], total[1:2], total[2:3]
    is_u, is_v, is_vort, is_adv = kind == 0, kind == 1, kind == 2, kind == 3
    seen = jnp.where(
        is_u,
        u,
        jnp.where(is_v, v, jnp.where(is_vort, slope_x - slope_y, u * slope_x + v * slope_y)),
    )
    misfit = wt_ref[...] * (seen - val_ref[...]) * scale
    zero = jnp.zeros_like(misfit)
    to_u = split(jnp.where(is_u, misfit, jnp.where(is_adv, misfit * slope_x, zero)))
    to_v = split(jnp.where(is_v, misfit, jnp.where(is_adv, misfit * slope_y, zero)))
    along_u = split(jnp.where(is_adv, misfit * u, zero))
    along_v = split(jnp.where(is_vort, misfit, zero))
    across = split(jnp.where(is_vort, -misfit, jnp.where(is_adv, misfit * v, zero)))

    high = rimb[...] * (along_u[0] + along_v[0])
    low = rimb[...] * (along_u[1] + along_v[1])
    rim = dot_nt(high, c0t[...]) + dot_nt(low, c0t[...])
    ftop[...] = rim[: GROUPS * EDGE].reshape(GROUPS, EDGE, NY)
    fbot[...] = rim[GROUPS * EDGE :].reshape(GROUPS, EDGE, NY)
    each(GROUPS, lambda g: begin(edges_back(g)))

    for half in range(2):
        lc[half * LINES : (half + 1) * LINES, :] = (
            r0b[0:LINES, :] * to_u[half] + r1b[0:LINES, :] * along_u[half]
        )
        lc[(2 + half) * LINES : (3 + half) * LINES, :] = (
            r0b[0:LINES, :] * to_v[half] + r1b[0:LINES, :] * along_v[half]
        )
        lh[half * LINES : (half + 1) * LINES, :] = r0b[0:LINES, :] * across[half]

    def scatter(step, _):
        at = pl.multiple_of(step * NB, NB)
        value = dot_nt(lc[...], c0t[pl.ds(at, NB), :])
        slope = dot_nt(lh[...], c1t[pl.ds(at, NB), :])
        grad[0, :, pl.ds(at, NB)] = (value[0:LINES] + value[LINES : 2 * LINES]) + (
            slope[0:LINES] + slope[LINES:]
        )
        grad[1, :, pl.ds(at, NB)] = value[2 * LINES : 3 * LINES] + value[3 * LINES :]
        return _

    lax.fori_loop(0, NY // NB, scatter, 0)

    def project(group):
        finish(edges_back(group))
        for h in range(PER):
            c = group * PER + h
            pieces = []
            row = lax.broadcasted_iota(I32, (RX, NY), 0)
            for k in range(LB):
                lev = c * LB + k
                at = pl.multiple_of(lev * RX, RX)
                gradients = []
                for w in range(2):
                    edge = w * (EDGE // 2) + h * LB + k
                    first = jnp.where(has_prev, gtop[group, edge : edge + 1, :], 0.0)
                    last = jnp.where(has_next, gbot[group, edge : edge + 1, :], 0.0)
                    gradients.append(
                        grad[w, pl.ds(at, RX), :]
                        + jnp.where(row == 0, first, jnp.where(row == RX - 1, last, 0.0))
                    )
                for m in range(M):
                    pieces.append(
                        gradients[0] * pert[m, 0, lev].astype(F32)
                        + gradients[1] * pert[m, 1, lev].astype(F32)
                    )
            high, low = split(jnp.concatenate(pieces, axis=0))
            at = pl.multiple_of(c * (ROWS * RX), ROWS * RX)
            value = dot(jnp.concatenate([high, low], axis=0), pyt[...])
            part[pl.ds(at, ROWS * RX), :] = value[: ROWS * RX] + value[ROWS * RX :]
            f = [part[pl.ds(at + i, ROWS, stride=RX), :] for i in range(RX)]
            taps = (0.125, 0.375, 0.625, 0.875, 0.875, 0.625, 0.375, 0.125)
            rows = {}
            for q in range(-1, R + 1):
                value = None
                for t, tap in enumerate(taps):
                    i = 4 * q - 2 + t
                    if 0 <= i < RX:
                        term = (diffuse * diffuse * tap) * f[i]
                        value = term if value is None else value + term
                rows[q] = inside(q, value)
            rows = one_pass(rows, -2, R + 1, inside)
            rows = one_pass(rows, -3, R + 2, inside)
            at = pl.multiple_of(c * ROWS, ROWS)
            for k in range(3):
                sdn[k, pl.ds(at, ROWS), :] = rows[k - 3]
                sup[k, pl.ds(at, ROWS), :] = rows[R + k]
            for k in range(LB):
                for r in range(R):
                    out_ref[pl.ds((c * LB + k) * R + r, M, stride=L * R), :] = rows[r][
                        k * M : (k + 1) * M
                    ]
            begin(rims_out(c))

    each(GROUPS, project)
    put_out = pltpu.make_async_copy(out_ref, out_hbm, local_sem.at[0])
    put_out.start()

    def collect(c):
        finish(rims_out(c))
        for k in range(LB):
            at = pl.multiple_of(c * ROWS + k * M, M)
            for r in range(R):
                value = 0.0
                if r < 3:
                    value = value + jnp.where(has_prev, qup[r, pl.ds(at, M), :], 0.0)
                if r >= R - 3:
                    value = value + jnp.where(has_next, qdn[r - (R - 3), pl.ds(at, M), :], 0.0)
                rest_ref[pl.ds((c * LB + k) * R + r, M, stride=L * R), :] = value

    each(CHUNKS, collect)
    put_rest = pltpu.make_async_copy(rest_ref, rest_hbm, local_sem.at[1])
    put_rest.start()
    put_out.wait()
    put_rest.wait()


def local(regions, members, alpha, perturbation, obs_cell, obs_kind, obs_value, obs_weight):
    any_space = pl.BlockSpec(memory_space=pl.ANY)
    row = (1, OBS)
    edge = pltpu.VMEM((GROUPS, EDGE, NY), F32)
    rows3 = pltpu.VMEM((3, M * L, C), F32)

    def stream(rows):
        one = pltpu.VMEM((rows, OBS), F32)
        return (
            one,
            pltpu.VMEM((YS - 1, rows, OBS), F32),
            one,
            pltpu.VMEM((ZS - 1, rows, OBS), F32),
        )

    out, rest = pl.pallas_call(
        functools.partial(kernel, 1.0 / math.sqrt(members), regions),
        out_shape=[jax.ShapeDtypeStruct((M * L * R, C), F32)] * 2,
        in_specs=[any_space] * 6,
        out_specs=[any_space] * 2,
        scratch_shapes=[
            pltpu.VMEM(row, I32),
            pltpu.VMEM(row, I32),
            pltpu.VMEM(row, F32),
            pltpu.VMEM(row, F32),
            pltpu.VMEM((M * L * R, C), F32),
            pltpu.VMEM((M * L * R, C), F32),
            pltpu.VMEM((M, 2, L, RX, NY), BF16),
            pltpu.VMEM((M, L * R, C), F32),
            pltpu.VMEM((R + 6, M * L, C), F32),
            pltpu.VMEM((M * L * RX, C), F32),
            pltpu.VMEM((NY, OBS), BF16),
            pltpu.VMEM((NY, OBS), BF16),
            pltpu.VMEM((LINES, OBS), F32),
            pltpu.VMEM((LINES, OBS), F32),
            pltpu.VMEM((LINES, OBS), BF16),
            pltpu.VMEM((LINES, OBS), BF16),
            pltpu.VMEM((2 * GROUPS * EDGE, OBS), F32),
            pltpu.VMEM((2 * GROUPS * EDGE, OBS), BF16),
            pltpu.VMEM((2 * C, NY), BF16),
            pltpu.VMEM((NY, C), BF16),
            pltpu.VMEM((4, LINES, NY), BF16),
            edge,
            edge,
            edge,
            edge,
            tuple(stream(rows) for rows in (3, 1)),
            pltpu.VMEM((4 * LINES, OBS), BF16),
            pltpu.VMEM((2 * LINES, OBS), BF16),
            edge,
            edge,
            edge,
            edge,
            pltpu.VMEM((2, LINES, NY), F32),
            rows3,
            rows3,
            rows3,
            rows3,
            pltpu.SemaphoreType.DMA((1 + CHUNKS + 4,)),
            pltpu.SemaphoreType.DMA((4 * CHUNKS + 4 * GROUPS + 12,)),
            pltpu.SemaphoreType.DMA((4 * CHUNKS + 4 * GROUPS + 12,)),
            pltpu.SemaphoreType.REGULAR,
        ],
        compiler_params=pltpu.CompilerParams(
            collective_id=0, has_side_effects=True, vmem_limit_bytes=62 * 1024 * 1024
        ),
    )(
        alpha.reshape(M, L * R, C),
        perturbation,
        obs_cell.reshape(row),
        obs_kind.reshape(row),
        obs_value.reshape(row),
        obs_weight.reshape(row),
    )
    return (out + rest).reshape(M, L, R, C)


def solution(mesh):
    regions, groups = mesh.shape["reg"], mesh.shape["mem"]
    return jax.shard_map(
        functools.partial(local, regions, M * groups),
        mesh=mesh,
        in_specs=(
            P("mem", None, "reg", None),
            P("mem", None, None, "reg", None),
            P("reg"),
            P("reg"),
            P("reg"),
            P("reg"),
        ),
        out_specs=P("mem", None, "reg", None),
        check_vma=False,
    )
```
